32 devices in a mesh: sub: 8 (over z, y), freq: 4 (over x, core).
Axes of the slice: x: 2, y: 2, z: 4, core: 2. Of those that a mesh axis runs over, the one named last changes fastest.
Arguments:
- freq_squared: float32 [16], P('freq'), may hold values from 0.05 to 1
- displacement: bfloat16 [1536, 2048], P('freq', 'sub'), may hold values from -6 to 6
- adjoint: bfloat16 [1536, 2048], P('freq', 'sub'), may hold values from -6 to 6
- incidence: int32 [24, 4], P('sub'), may hold values from 0 to 15, as said below
- block_count: int32 [24], P('sub'), may hold values from 1 to 4, as said below
- mode_count: int32 [24], P('sub'), may hold values from 1 to 128, as said below
- stiffness: bfloat16 [24, 512, 512], P('sub'), may hold values from -0.25 to 0.25
- mass_matrix: bfloat16 [24, 512, 512], P('sub'), may hold values from -0.25 to 0.25
- coupling: bfloat16 [24, 128, 512], P('sub'), may hold values from -0.25 to 0.25
- eigenvalues: float32 [24, 128], P('sub'), may hold values from 1.5 to 20
- flexibility: float32 [24, 512], P('sub'), may hold values from 0.2 to 1
Outputs:
- interface_residual: float32 [1536, 2048], P('freq', 'sub')
- eigen_gradient: float32 [24, 128], P('sub')
- coupling_gradient: float32 [24, 128, 512], P('sub', None, 'freq')
- flexibility_gradient: float32 [24, 512], P('sub')
The draws below stay inside these ranges and needn't reach their ends.
Inputs may be any that keep to these rules, and one draw needn't show every extreme that they name: `incidence`: every slot, live or not, names a block owned by the index of sub that holds the substructure or one at most 1 indices away (block b is owned by index b // 2). The first substructure of every index of sub touches, in live slots, a block of the owner 1 indices below and one 1 above wherever such owners exist. A substructure may name one block in several slots. `block_count`: the first substructure of every index of sub has 4 live slots. Modes j >= mode_count[s] are absent. The first substructure of every index of sub keeps 128 modes.
All inputs are finite; a program needn't handle non-finite values.
Results may differ from the reference program's by a relative error of at most 0.0029.
Values may be sent and summed in bfloat16 or wider, within the bound.
A program may use at most 64 MiB of HBM per device.

```python
import math
import jax
import jax.numpy as jnp
from jax import lax

B = 128
KMAX = 4
M = 128
F = 16
LC = 96
SUB_DEV = 3
BLK_DEV = 2
WIN = 1
KB = 512
S = 24
NB = 16


def draw_incidence(key, part):
    sub_ids = jnp.arange(S)
    device_ids = sub_ids // SUB_DEV
    first_key, second_key = jax.random.split(jax.random.fold_in(key, 11))
    shifts = jax.random.randint(first_key, (S, KMAX), -WIN, WIN + 1)
    slot_ids = jnp.arange(KMAX)[None, :]
    forced = jnp.where(slot_ids == 0, -WIN, jnp.where(slot_ids == 1, WIN, shifts))
    leading = (sub_ids % SUB_DEV == 0)[:, None]
    shifts = jnp.where(leading, forced, shifts)
    owners = jnp.clip(device_ids[:, None] + shifts, 0, NB // BLK_DEV - 1)
    local_block = jax.random.randint(second_key, (S, KMAX), 0, BLK_DEV)
    return (owners * BLK_DEV + local_block).astype(jnp.int32)


def draw_block_count(key, part):
    sub_ids = jnp.arange(S)
    counts = jax.random.randint(jax.random.fold_in(key, 23), (S,), 1, KMAX + 1)
    return jnp.where(sub_ids % SUB_DEV == 0, KMAX, counts).astype(jnp.int32)


def draw_mode_count(key, part):
    sub_ids = jnp.arange(S)
    counts = jax.random.randint(jax.random.fold_in(key, 37), (S,), M // 4, M + 1)
    return jnp.where(sub_ids % SUB_DEV == 0, M, counts).astype(jnp.int32)


def shard_levels(key, dims, shards, smallest, largest):
    gain = 1.0
    for dim, parts in shards:
        steps = jax.random.uniform(jax.random.fold_in(jax.random.fold_in(key, 6), dim), (parts,), jnp.float32, smallest / len(shards), largest / len(shards))
        gain = gain * jnp.repeat(jnp.exp(steps), dims[dim] // parts).reshape((-1,) + (1,) * (len(dims) - 1 - dim))
    return gain


def noise(rng, shape, deviation, most, cuts=(), dtype=jnp.bfloat16):
    level = shard_levels(rng, shape, cuts, -0.22, 0.18) if cuts else 1.0
    array = jax.random.normal(rng, shape, jnp.float32) * deviation * level
    return jnp.minimum(jnp.maximum(array, -most), most).astype(dtype)


def setup_inputs(seed: int = 0) -> dict:
    streams_of = jax.random.split(jax.random.key(seed), 12)
    freq_squared = jnp.clip(0.05 + 0.95 * jax.random.uniform(streams_of[0], (F,), jnp.float32) ** shard_levels(streams_of[0], (F,), ((0, 4),), -0.2, 0.2), 0.05, 1.0)
    displacement = noise(streams_of[1], (F * LC, NB * B), 1.0, 6.0, ((0, 4), (1, 8)))
    adjoint = noise(streams_of[2], (F * LC, NB * B), 1.0, 6.0, ((0, 4), (1, 8)))
    incidence = draw_incidence(jax.random.fold_in(streams_of[11], 71), 0)
    block_count = draw_block_count(jax.random.fold_in(streams_of[11], 71), 0)
    mode_count = draw_mode_count(jax.random.fold_in(streams_of[11], 71), 0)
    stiffness = noise(streams_of[6], (S, KB, KB), KB ** -0.5, 0.25, ((0, 8),))
    mass_matrix = noise(streams_of[7], (S, KB, KB), KB ** -0.5, 0.25, ((0, 8),))
    coupling = noise(streams_of[8], (S, M, KB), KB ** -0.5, 0.25, ((0, 8),))
    eigenvalues = jnp.clip(jnp.exp(math.log(20.0) - 2.5902672 * jax.random.uniform(streams_of[9], (S, M), jnp.float32) ** shard_levels(streams_of[9], (S, M), ((0, 8),), -0.2, 0.2)), 1.5, 20.0)
    flexibility = jnp.clip(0.2 + 0.8 * jax.random.uniform(streams_of[10], (S, KB), jnp.float32) ** shard_levels(streams_of[10], (S, KB), ((0, 8),), -0.2, 0.2), 0.2, 1.0)
    return dict(freq_squared=freq_squared, displacement=displacement, adjoint=adjoint, incidence=incidence, block_count=block_count, mode_count=mode_count, stiffness=stiffness, mass_matrix=mass_matrix, coupling=coupling, eigenvalues=eigenvalues, flexibility=flexibility)


def reference(freq_squared, displacement, adjoint, incidence, block_count, mode_count, stiffness, mass_matrix, coupling, eigenvalues, flexibility):
    columns = displacement.shape[0]
    squares = jnp.repeat(freq_squared, LC)
    fourth = squares * squares
    adjoint_blocks = adjoint.reshape(columns, NB, B)
    displacement_blocks = displacement.reshape(columns, NB, B)
    slot_range = jnp.arange(KMAX)
    mode_range = jnp.arange(M)

    def one_substructure(summed, per_sub):
        blocks, live_count, mode_total, stiff_sub, mass_sub, couple_sub, eigen_sub, flex_sub = per_sub
        live_slot = slot_range < live_count
        slot_mask = live_slot.astype(jnp.bfloat16)[None, :, None]
        adjoint_sub = (jnp.take(adjoint_blocks, blocks, axis=1) * slot_mask).reshape(columns, KB)
        displacement_sub = (jnp.take(displacement_blocks, blocks, axis=1) * slot_mask).reshape(columns, KB)
        modal_adjoint = jnp.dot(adjoint_sub, couple_sub.T, preferred_element_type=jnp.float32)
        modal_displacement = jnp.dot(displacement_sub, couple_sub.T, preferred_element_type=jnp.float32)
        inverse = 1.0 / (eigen_sub[None, :] - squares[:, None])
        factor = jnp.where(mode_range[None, :] < mode_total, fourth[:, None] * inverse, jnp.float32(0.0))
        weight_adjoint = (factor * modal_adjoint).astype(jnp.bfloat16)
        weight_displacement = (factor * modal_displacement).astype(jnp.bfloat16)
        eigen_part = jnp.sum(factor * inverse * modal_adjoint * modal_displacement, axis=0)
        flex_part = -jnp.sum(fourth[:, None] * adjoint_sub.astype(jnp.float32) * displacement_sub.astype(jnp.float32), axis=0)
        couple_part = -(jnp.dot(weight_adjoint.T, displacement_sub, preferred_element_type=jnp.float32)
                        + jnp.dot(weight_displacement.T, adjoint_sub, preferred_element_type=jnp.float32))
        response = (jnp.dot(adjoint_sub, stiff_sub.T, preferred_element_type=jnp.float32)
                    - squares[:, None] * jnp.dot(adjoint_sub, mass_sub.T, preferred_element_type=jnp.float32)
                    - jnp.dot(weight_adjoint, couple_sub, preferred_element_type=jnp.float32)
                    - fourth[:, None] * flex_sub[None, :] * adjoint_sub.astype(jnp.float32))
        for slot_index in range(KMAX):
            first_col = (blocks[slot_index] * B).astype(jnp.int32)
            current = lax.dynamic_slice_in_dim(summed, first_col, B, 1)
            added = response[:, slot_index * B:(slot_index + 1) * B] * live_slot[slot_index].astype(jnp.float32)
            summed = lax.dynamic_update_slice_in_dim(summed, current + added, first_col, 1)
        return summed, (eigen_part, flex_part, couple_part)

    initial = jnp.zeros((columns, NB * B), jnp.float32)
    summed, outputs = lax.scan(one_substructure, initial, (incidence, block_count, mode_count, stiffness, mass_matrix, coupling, eigenvalues, flexibility))
    eigen_gradient, flexibility_gradient, coupling_gradient = outputs
    return summed, eigen_gradient, coupling_gradient, flexibility_gradient
```

```python
import functools

import jax
import jax.numpy as jnp
from jax import lax
from jax.experimental import pallas as pl
from jax.experimental.pallas import tpu as pltpu
from jax.sharding import PartitionSpec as P

MESH = pl.DeviceIdType.MESH
NT = (((1,), (1,)), ((), ()))
NN = (((1,), (0,)), ((), ()))
TN = (((0,), (0,)), ((), ()))


def dot(a, b, dims):
    return lax.dot_general(a, b, dims, preferred_element_type=jnp.float32)


def group_of(chunks):
    return 2 if chunks % 2 == 0 else 1


def pair_of(n_freq):
    return 2 if n_freq % 2 == 0 else 1


def fold(x):
    return jnp.sum(x.reshape(x.shape[0] // 8, 8, x.shape[1]), axis=0)


def kernel(
    n_sub,
    n_freq,
    chunks,
    freq_hbm,
    inc_hbm,
    count_hbm,
    mode_hbm,
    eig_hbm,
    flex_hbm,
    adj_hbm,
    dis_hbm,
    stiff_hbm,
    mass_hbm,
    coup_hbm,
    out_ref,
    eig_out,
    cg_out_ref,
    flex_out,
    *scratch,
):
    group = group_of(chunks)
    halves = chunks // group
    win_a = scratch[:halves]
    win_d = scratch[halves : halves + chunks]
    (
        freq_ref,
        inc_ref,
        count_ref,
        mode_ref,
        block_tab,
        order_tab,
        last_tab,
        keep_tab,
        eig_ref,
        flex_ref,
        stiff,
        mass,
        coup,
        resp,
        runs,
        modal,
        weight_a,
        near_acc,
        far_out,
        far_in,
        near_out,
        near_in,
        flex_acc,
        eig_acc,
        pack,
        grad,
        first_out,
        first_in,
        second_out,
        second_in,
        own_sem,
        weight_sem,
        small_sem,
        near_send,
        near_recv,
        relay_send,
        relay_recv,
        far_send,
        far_recv,
        back_send,
        back_recv,
        pack_send,
        pack_recv,
        first_send,
        first_recv,
        second_send,
        second_recv,
    ) = scratch[halves + chunks :]
    sub_here, slots = inc_ref.shape
    columns, owned_cells = adj_hbm.shape
    rows = columns // chunks
    kb = stiff.shape[1]
    block = kb // slots
    owned = owned_cells // block
    modes = coup.shape[1]
    part = kb // n_freq
    n_slots = sub_here * slots
    spare = 3 * owned

    me = lax.axis_index("sub")
    fr = lax.axis_index("freq")
    odd = me % 2
    step = 2 - 4 * odd
    partner = me + 1 - 2 * odd
    target = me + step
    source = me - step
    has_target = (target >= 0) & (target < n_sub)
    has_source = (source >= 0) & (source < n_sub)
    target = jnp.clip(target, 0, n_sub - 1)
    source = jnp.clip(source, 0, n_sub - 1)

    weight_copies = [
        pltpu.make_async_copy(hbm, vmem, weight_sem.at[i])
        for i, (hbm, vmem) in enumerate(((coup_hbm, coup), (stiff_hbm, stiff), (mass_hbm, mass)))
    ]
    small_copies = [
        pltpu.make_async_copy(hbm, local, small_sem.at[i])
        for i, (hbm, local) in enumerate(
            (
                (freq_hbm, freq_ref),
                (inc_hbm, inc_ref),
                (count_hbm, count_ref),
                (mode_hbm, mode_ref),
                (eig_hbm, eig_ref),
                (flex_hbm, flex_ref),
            )
        )
    ]

    def here(c):
        return pl.ds(c * rows, rows)

    def within(c):
        return pl.ds((c % group) * rows, rows)

    def slab(t, c, place):
        blocks = pl.ds(place * owned, owned)
        if t == 0:
            return win_a[c // group].at[blocks, within(c), :]
        return win_d[c].at[blocks]

    def cell(t, c, inner):
        if t == 0:
            return win_a[c // group].at[inner, within(c), :]
        return win_d[c].at[inner]

    def remote(src, dst, send, recv, sub, freq):
        return pltpu.make_async_remote_copy(
            src_ref=src,
            dst_ref=dst,
            send_sem=send,
            recv_sem=recv,
            device_id=(sub, freq),
            device_id_type=MESH,
        )

    own_copies = [
        [
            [
                pltpu.make_async_copy(
                    ref.at[here(c), pl.ds(inner * block, block)],
                    cell(t, c, inner),
                    own_sem.at[t, c, inner],
                )
                for inner in range(owned)
            ]
            for c in range(chunks)
        ]
        for t, ref in enumerate((adj_hbm, dis_hbm))
    ]
    near_copies = [
        [
            remote(
                slab(t, c, 0), slab(t, c, 1), near_send.at[t, c], near_recv.at[t, c], partner, fr
            )
            for c in range(chunks)
        ]
        for t in range(2)
    ]
    relay_copies = [
        [
            remote(
                slab(t, c, 1), slab(t, c, 2), relay_send.at[t, c], relay_recv.at[t, c], target, fr
            )
            for c in range(chunks)
        ]
        for t in range(2)
    ]
    far_copies = [
        remote(far_out.at[c], far_in.at[c], far_send.at[c], far_recv.at[c], source, fr)
        for c in range(chunks)
    ]
    back_copies = [
        remote(near_out.at[c], near_in.at[c], back_send.at[c], back_recv.at[c], partner, fr)
        for c in range(chunks)
    ]
    peers = [(fr + d) % n_freq for d in range(n_freq)]
    pack_copies = [
        remote(pack.at[0], pack.at[d], pack_send.at[d], pack_recv.at[d], me, peers[d])
        for d in range(1, n_freq)
    ]
    pair = pair_of(n_freq)
    teams = n_freq // pair
    team = fr // pair
    rank = fr % pair
    other = (rank + 1) % pair
    first_copies = [
        remote(
            first_out.at[s, other],
            first_in.at[s],
            first_send.at[s],
            first_recv.at[s],
            me,
            team * pair + other,
        )
        for s in range(sub_here)
    ]
    away = [(team + d) % teams for d in range(teams)]
    second_copies = [
        [
            remote(
                second_out.at[s, d],
                second_in.at[s, d],
                second_send.at[s, d],
                second_recv.at[s, d],
                me,
                away[d] * pair + rank,
            )
            for d in range(1, teams)
        ]
        for s in range(sub_here)
    ]

    barrier = pltpu.get_barrier_semaphore()

    def greet(sub, freq):
        pl.semaphore_signal(barrier, inc=1, device_id=(sub, freq), device_id_type=MESH)

    greet(partner, fr)
    for d in range(1, n_freq):
        greet(me, peers[d])

    @pl.when(has_target)
    def _():
        greet(target, fr)

    @pl.when(has_source)
    def _():
        greet(source, fr)

    for copies in own_copies[0] + own_copies[1]:
        for copy in copies:
            copy.start()
    for copy in small_copies + weight_copies:
        copy.start()

    @pl.when(jnp.logical_not(has_target))
    def _():
        far_in[...] = jnp.zeros_like(far_in)

    for ref in (*win_a, *win_d):
        ref[spare] = jnp.zeros(ref.shape[1:], ref.dtype)
    runs[n_slots] = jnp.zeros(runs.shape[1:], runs.dtype)
    flex_acc[...] = jnp.zeros_like(flex_acc)
    eig_acc[...] = jnp.zeros_like(eig_acc)

    with jax.named_scope("barrier"):
        pl.semaphore_wait(
            barrier, n_freq + has_target.astype(jnp.int32) + has_source.astype(jnp.int32)
        )
    with jax.named_scope("near"):
        for t in range(2):
            for c in range(chunks):
                for copy in own_copies[t][c]:
                    copy.wait()
                near_copies[t][c].start()

    def relay(t, c):
        with jax.named_scope(f"relay{t}{c}"):
            near_copies[t][c].wait_recv()

            @pl.when(has_target)
            def _():
                relay_copies[t][c].start()

    def relayed(t, c):
        with jax.named_scope(f"relayed{t}{c}"):

            @pl.when(has_source)
            def _():
                relay_copies[t][c].wait_recv()

    with jax.named_scope("small"):
        for copy in small_copies:
            copy.wait()

    one, none = jnp.int32(1), jnp.int32(0)
    keys = []
    for s in range(sub_here):
        for k in range(slots):
            named = inc_ref[s, k]
            live = k < count_ref[s]
            key = jnp.int32(spare)
            for w, owner in enumerate((me, partner, me - 1 + 2 * odd)):
                for inner in range(owned):
                    hit = live & (named == owner * owned + inner)
                    key = jnp.where(hit, jnp.int32(w * owned + inner), key)
            block_tab[s * slots + k] = key
            keys.append(key)

    def count(tests):
        total = none
        for test in tests:
            total = total + jnp.where(test, one, none)
        return total

    ranks = [
        count(
            [keys[j] <= keys[i] for j in range(i)]
            + [keys[j] < keys[i] for j in range(i + 1, n_slots)]
        )
        for i in range(n_slots)
    ]
    before = None
    for r in range(n_slots):
        index, key = none, none
        for i in range(n_slots):
            chosen = ranks[i] == r
            index = jnp.where(chosen, jnp.int32(i), index)
            key = jnp.where(chosen, keys[i], key)
        order_tab[r] = index
        if r:
            keep_tab[r] = jnp.where(key == before, jnp.float32(1), jnp.float32(0))
        before = key
    for b in range(3 * owned):
        hits = count([key == b for key in keys])
        upto = count([key <= b for key in keys])
        last_tab[b] = jnp.where(hits > 0, upto - 1, jnp.int32(n_slots))

    for c in range(chunks):
        relay(0, c)

    def gather(ref, s, where):
        return jnp.concatenate(
            [ref[block_tab[s * slots + k], where, :] for k in range(slots)],
            axis=1,
        )

    def scales(c, s):
        w2 = freq_ref[c]
        w4 = w2 * w2
        inverse = 1.0 / (eig_ref[pl.ds(s, 1), :] - w2)
        mode_index = lax.broadcasted_iota(jnp.int32, (1, modes), 1)
        factor = jnp.where(mode_index < mode_ref[s], w4 * inverse, 0.0)
        return w2, w4, inverse, factor

    tile = 2 * block if slots % 2 == 0 else block

    def respond(p, s):
        a = gather(win_a[p], s, pl.ds(0, group * rows))
        couple = coup[s]
        ma = dot(a, couple, NT)
        parts = []
        for i in range(group):
            c = p * group + i
            factor = scales(c, s)[3]
            piece = ma[i * rows : (i + 1) * rows]
            modal[s, here(c), :] = piece
            parts.append((-factor * piece).astype(jnp.bfloat16))
        wa = jnp.concatenate(parts, axis=0)
        weight_a[s, pl.ds(p * group * rows, group * rows), :] = wa
        for n in range(kb // tile):
            lanes = slice(n * tile, (n + 1) * tile)
            plain = dot(a, stiff[s, lanes, :], NT) + dot(wa, couple[:, lanes], NN)
            inert = dot(a, mass[s, lanes, :], NT)
            for i in range(group):
                c = p * group + i
                w2, w4 = scales(c, s)[:2]
                span = slice(i * rows, (i + 1) * rows)
                value = (
                    plain[span]
                    - w2 * inert[span]
                    - (w4 * flex_ref[s : s + 1, lanes]) * a[span, lanes].astype(jnp.float32)
                )
                for k in range(tile // block):
                    slot = s * slots + n * (tile // block) + k
                    resp[slot, within(c), :] = value[:, k * block : (k + 1) * block]

    def spread(c):
        with jax.named_scope(f"spread{c}"):
            total = None
            for r in range(n_slots):
                term = resp[order_tab[r], within(c), :]
                total = term if total is None else total * keep_tab[r] + term
                runs[r] = total
            for place in (2, 1, 0):
                for inner in range(owned):
                    value = runs[last_tab[place * owned + inner]]
                    lane = pl.ds(inner * block, block)
                    if place == 0:
                        out_ref[here(c), lane] = value
                    elif place == 1:
                        near_acc[c, :, lane] = value
                    else:
                        far_out[c, :, lane] = value.astype(far_out.dtype)
                if place == 2:

                    @pl.when(has_source)
                    def _():
                        far_copies[c].start()

    steps = halves * sub_here
    passed = 0
    for p in range(halves):
        for i in range(group):
            relayed(0, p * group + i)
        if p == 0:
            with jax.named_scope("weights"):
                for copy in weight_copies:
                    copy.wait()
        for s in range(sub_here):
            with jax.named_scope(f"respond{p}{s}"):
                respond(p, s)
            due = min(chunks, ((2 * (p * sub_here + s) + 3) * chunks) // (2 * steps))
            while passed < due:
                relay(1, passed)
                passed += 1
        for i in range(group):
            spread(p * group + i)
    while passed < chunks:
        relay(1, passed)
        passed += 1

    def modal_part(c, s):
        ref = win_d[c]
        w2, w4, inverse, factor = scales(c, s)
        d = gather(ref, s, pl.ds(0, rows))
        a = gather(win_a[c // group], s, within(c))
        md = dot(d, coup[s], NT)
        wd = (-factor * md).astype(jnp.bfloat16)
        eig_acc[s] += (factor * inverse) * fold(modal[s, here(c), :] * md)
        left = jnp.concatenate([weight_a[s, here(c), :], wd], axis=0)
        right = jnp.concatenate([d, a], axis=0)
        value = dot(left, right, TN)
        if c:
            value = value + grad[s]
        if c + 1 < chunks:
            grad[s] = value
            return
        grad[s] = value
        for j in range(n_freq):
            first_out[s, j % pair, j // pair] = value[:, j * part : (j + 1) * part].astype(
                first_out.dtype
            )
        if pair > 1:
            first_copies[s].start()

    def flex_part(c):
        w4 = freq_ref[c] * freq_ref[c]
        for place in range(3):
            for inner in range(owned):
                b = place * owned + inner
                a = win_a[c // group][b, within(c), :].astype(jnp.float32)
                d = win_d[c][b].astype(jnp.float32)
                flex_acc[b] += -w4 * fold(a * d)

    def combine(c):
        with jax.named_scope(f"combine{c}"):

            @pl.when(has_target)
            def _():
                far_copies[c].wait_recv()

            near_out[c] = (near_acc[c] + far_in[c].astype(jnp.float32)).astype(near_out.dtype)
            back_copies[c].start()

    def finish(c):
        with jax.named_scope(f"finish{c}"):
            back_copies[c].wait_recv()
            out_ref[here(c), :] += near_in[c].astype(jnp.float32)

    combined = 0
    for c in range(chunks):
        relayed(1, c)
        with jax.named_scope(f"modal{c}"):
            for s in range(sub_here):
                modal_part(c, s)
        with jax.named_scope(f"flex{c}"):
            flex_part(c)
        if 1 <= c < chunks - 1:
            combine(combined)
            combined += 1

    with jax.named_scope("pack"):
        wide = max(block, modes)
        pack[0] = jnp.zeros(pack.shape[1:], pack.dtype)
        for s in range(sub_here):
            base = s * (slots + 1)
            for k in range(slots):
                pack[0, base + k : base + k + 1, 0:block] = jnp.sum(
                    flex_acc[block_tab[s * slots + k]], axis=0, keepdims=True
                )
            pack[0, base + slots : base + slots + 1, 0:modes] = jnp.sum(
                eig_acc[s], axis=0, keepdims=True
            )
        for copy in pack_copies:
            copy.start()

    while combined < chunks:
        combine(combined)
        combined += 1

    for s in range(sub_here):
        with jax.named_scope(f"second{s}"):
            if pair > 1:
                first_copies[s].wait_recv()
            for d in range(1, teams):
                j = away[d]
                lane = pl.ds(pl.multiple_of((j * pair + rank) * part, part), part)
                value = grad[s, :, lane]
                if pair > 1:
                    value = value + first_in[s, j].astype(jnp.float32)
                second_out[s, d] = value.astype(second_out.dtype)
            for copy in second_copies[s]:
                copy.start()

    for c in range(chunks):
        finish(c)

    with jax.named_scope("packwait"):
        for copy in pack_copies:
            copy.wait_recv()
    total = None
    for i in range(n_freq):
        term = pack[(fr - i + n_freq) % n_freq]
        total = term if total is None else total + term
    for s in range(sub_here):
        base = s * (slots + 1)
        for k in range(slots):
            flex_out[s : s + 1, k * block : (k + 1) * block] = total[
                base + k : base + k + 1, 0:block
            ]
        eig_out[s : s + 1, :] = total[base + slots : base + slots + 1, 0:modes]
    for s in range(sub_here):
        with jax.named_scope(f"grad{s}"):
            lane = pl.ds(pl.multiple_of(fr * part, part), part)
            value = grad[s, :, lane]
            if pair > 1:
                value = value + first_in[s, team].astype(jnp.float32)
            for d in range(1, teams):
                second_copies[s][d - 1].wait_recv()
                value = value + second_in[s, d].astype(jnp.float32)
            cg_out_ref[s] = value

    with jax.named_scope("end"):
        for c in range(chunks):
            for t in range(2):
                near_copies[t][c].wait_send()
            back_copies[c].wait_send()

        @pl.when(has_target)
        def _():
            for c in range(chunks):
                for t in range(2):
                    relay_copies[t][c].wait_send()

        @pl.when(has_source)
        def _():
            for c in range(chunks):
                far_copies[c].wait_send()

        for copy in pack_copies:
            copy.wait_send()
        for s in range(sub_here):
            if pair > 1:
                first_copies[s].wait_send()
            for copy in second_copies[s]:
                copy.wait_send()


def write_out(*refs):
    count = len(refs) // 2
    sems = refs[-1]
    copies = [
        pltpu.make_async_copy(refs[i], refs[count + i], sems.at[i]) for i in range(count)
    ]
    for copy in copies:
        copy.start()
    for copy in copies:
        copy.wait()


def shards(
    n_sub,
    n_freq,
    freq_squared,
    displacement,
    adjoint,
    incidence,
    block_count,
    mode_count,
    stiffness,
    mass_matrix,
    coupling,
    eigenvalues,
    flexibility,
):
    sub_here, slots = incidence.shape
    columns, owned_cells = displacement.shape
    chunks = freq_squared.shape[0]
    rows = columns // chunks
    kb = stiffness.shape[1]
    block = kb // slots
    owned = owned_cells // block
    modes = coupling.shape[1]
    part = kb // n_freq
    group = group_of(chunks)
    pair = pair_of(n_freq)
    teams = n_freq // pair
    n_slots = sub_here * slots
    pack_rows = -(-(sub_here * (slots + 1)) // 8) * 8
    bf16, f32, i32 = jnp.bfloat16, jnp.float32, jnp.int32
    vmem = pl.BlockSpec(memory_space=pltpu.VMEM)
    hbm = pl.BlockSpec(memory_space=pltpu.HBM)
    dma = pltpu.SemaphoreType.DMA
    slab = (chunks, rows, owned_cells)
    scratch = (
        [
            pltpu.VMEM((3 * owned + 1, group * rows, block), bf16)
            for _ in range(chunks // group)
        ]
        + [pltpu.VMEM((3 * owned + 1, rows, block), bf16) for _ in range(chunks)]
        + [
            pltpu.SMEM(freq_squared.shape, f32),
            pltpu.SMEM(incidence.shape, i32),
            pltpu.SMEM(block_count.shape, i32),
            pltpu.SMEM(mode_count.shape, i32),
            pltpu.SMEM((n_slots,), i32),
            pltpu.SMEM((n_slots,), i32),
            pltpu.SMEM((3 * owned,), i32),
            pltpu.SMEM((n_slots,), f32),
            pltpu.VMEM(eigenvalues.shape, f32),
            pltpu.VMEM(flexibility.shape, f32),
            pltpu.VMEM(stiffness.shape, bf16),
            pltpu.VMEM(mass_matrix.shape, bf16),
            pltpu.VMEM(coupling.shape, bf16),
            pltpu.VMEM((n_slots, group * rows, block), f32),
            pltpu.VMEM((n_slots + 1, rows, block), f32),
            pltpu.VMEM((sub_here, columns, modes), f32),
            pltpu.VMEM((sub_here, columns, modes), bf16),
            pltpu.VMEM(slab, f32),
            pltpu.VMEM(slab, bf16),
            pltpu.VMEM(slab, bf16),
            pltpu.VMEM(slab, bf16),
            pltpu.VMEM(slab, bf16),
            pltpu.VMEM((3 * owned + 1, 8, block), f32),
            pltpu.VMEM((sub_here, 8, modes), f32),
            pltpu.VMEM((n_freq, pack_rows, max(block, modes)), f32),
            pltpu.VMEM((sub_here, modes, kb), f32),
            pltpu.VMEM((sub_here, pair, teams, modes, part), bf16),
            pltpu.VMEM((sub_here, teams, modes, part), bf16),
            pltpu.VMEM((sub_here, teams, modes, part), bf16),
            pltpu.VMEM((sub_here, teams, modes, part), bf16),
            dma((2, chunks, owned)),
            dma((3,)),
            dma((6,)),
            dma((2, chunks)),
            dma((2, chunks)),
            dma((2, chunks)),
            dma((2, chunks)),
            dma((chunks,)),
            dma((chunks,)),
            dma((chunks,)),
            dma((chunks,)),
            dma((n_freq,)),
            dma((n_freq,)),
            dma((sub_here,)),
            dma((sub_here,)),
            dma((sub_here, teams)),
            dma((sub_here, teams)),
        ]
    )
    results = pl.pallas_call(
        functools.partial(kernel, n_sub, n_freq, chunks),
        out_shape=(
            jax.ShapeDtypeStruct((columns, owned_cells), f32),
            jax.ShapeDtypeStruct((sub_here, modes), f32),
            jax.ShapeDtypeStruct((sub_here, modes, part), f32),
            jax.ShapeDtypeStruct((sub_here, kb), f32),
        ),
        in_specs=[hbm] * 11,
        out_specs=(vmem,) * 4,
        scratch_shapes=scratch,
        compiler_params=pltpu.CompilerParams(
            collective_id=0, has_side_effects=True, vmem_limit_bytes=48 * 1024 * 1024
        ),
    )(
        *(
            pltpu.with_memory_space_constraint(x, pltpu.HBM)
            for x in (
                freq_squared,
                incidence,
                block_count,
                mode_count,
                eigenvalues,
                flexibility,
                adjoint,
                displacement,
                stiffness,
                mass_matrix,
                coupling,
            )
        )
    )
    return pl.pallas_call(
        write_out,
        out_shape=tuple(jax.ShapeDtypeStruct(x.shape, x.dtype) for x in results),
        in_specs=[vmem] * 4,
        out_specs=(pl.BlockSpec(memory_space=pltpu.HBM),) * 4,
        scratch_shapes=[dma((4,))],
        compiler_params=pltpu.CompilerParams(vmem_limit_bytes=4 * 1024 * 1024),
    )(*results)


def solution(mesh):
    in_specs = (
        P("freq"),
        P("freq", "sub"),
        P("freq", "sub"),
        P("sub", None),
        P("sub"),
        P("sub"),
        P("sub", None, None),
        P("sub", None, None),
        P("sub", None, None),
        P("sub", None),
        P("sub", None),
    )
    out_specs = (P("freq", "sub"), P("sub", None), P("sub", None, "freq"), P("sub", None))
    body = functools.partial(shards, mesh.shape["sub"], mesh.shape["freq"])
    return jax.shard_map(body, mesh=mesh, in_specs=in_specs, out_specs=out_specs, check_vma=False)
```

```python
import functools

import jax
import jax.numpy as jnp
from jax import lax
from jax.experimental import pallas as pl
from jax.experimental.pallas import tpu as pltpu
from jax.sharding import PartitionSpec as P

MESH = pl.DeviceIdType.MESH
NT = (((1,), (1,)), ((), ()))
NN = (((1,), (0,)), ((), ()))
TN = (((0,), (0,)), ((), ()))


def dot(a, b, dims):
    return lax.dot_general(a, b, dims, preferred_element_type=jnp.float32)


def group_of(chunks):
    return 2 if chunks % 2 == 0 else 1


def pair_of(n_freq):
    return 2 if n_freq % 2 == 0 else 1


def fold(x):
    return jnp.sum(x.reshape(x.shape[0] // 8, 8, x.shape[1]), axis=0)


def kernel(
    n_sub,
    n_freq,
    chunks,
    freq_hbm,
    inc_hbm,
    count_hbm,
    mode_hbm,
    eig_hbm,
    flex_hbm,
    adj_hbm,
    dis_hbm,
    stiff_hbm,
    mass_hbm,
    coup_hbm,
    out_ref,
    eig_out,
    cg_out_ref,
    flex_out,
    *scratch,
):
    group = group_of(chunks)
    halves = chunks // group
    win_a = scratch[:halves]
    win_d = scratch[halves : halves + chunks]
    (
        freq_ref,
        inc_ref,
        count_ref,
        mode_ref,
        block_tab,
        order_tab,
        last_tab,
        keep_tab,
        eig_ref,
        flex_ref,
        stiff,
        mass,
        coup,
        resp,
        runs,
        modal,
        weight_a,
        near_acc,
        far_out,
        far_in,
        near_out,
        near_in,
        flex_acc,
        eig_acc,
        pack,
        grad,
        first_out,
        first_in,
        second_out,
        second_in,
        own_sem,
        weight_sem,
        small_sem,
        near_send,
        near_recv,
        relay_send,
        relay_recv,
        far_send,
        far_recv,
        back_send,
        back_recv,
        pack_send,
        pack_recv,
        first_send,
        first_recv,
        second_send,
        second_recv,
    ) = scratch[halves + chunks :]
    sub_here, slots = inc_ref.shape
    columns, owned_cells = adj_hbm.shape
    rows = columns // chunks
    kb = stiff.shape[1]
    block = kb // slots
    owned = owned_cells // block
    modes = coup.shape[1]
    part = kb // n_freq
    n_slots = sub_here * slots
    spare = 3 * owned

    me = lax.axis_index("sub")
    fr = lax.axis_index("freq")
    odd = me % 2
    step = 2 - 4 * odd
    partner = me + 1 - 2 * odd
    target = me + step
    source = me - step
    has_target = (target >= 0) & (target < n_sub)
    has_source = (source >= 0) & (source < n_sub)
    target = jnp.clip(target, 0, n_sub - 1)
    source = jnp.clip(source, 0, n_sub - 1)

    weight_copies = [
        pltpu.make_async_copy(hbm, vmem, weight_sem.at[i])
        for i, (hbm, vmem) in enumerate(((coup_hbm, coup), (stiff_hbm, stiff), (mass_hbm, mass)))
    ]
    small_copies = [
        pltpu.make_async_copy(hbm, local, small_sem.at[i])
        for i, (hbm, local) in enumerate(
            (
                (freq_hbm, freq_ref),
                (inc_hbm, inc_ref),
                (count_hbm, count_ref),
                (mode_hbm, mode_ref),
                (eig_hbm, eig_ref),
                (flex_hbm, flex_ref),
            )
        )
    ]

    def here(c):
        return pl.ds(c * rows, rows)

    def within(c):
        return pl.ds((c % group) * rows, rows)

    def slab(t, c, place):
        blocks = pl.ds(place * owned, owned)
        if t == 0:
            return win_a[c // group].at[blocks, within(c), :]
        return win_d[c].at[blocks]

    def cell(t, c, inner):
        if t == 0:
            return win_a[c // group].at[inner, within(c), :]
        return win_d[c].at[inner]

    def remote(src, dst, send, recv, sub, freq):
        return pltpu.make_async_remote_copy(
            src_ref=src,
            dst_ref=dst,
            send_sem=send,
            recv_sem=recv,
            device_id=(sub, freq),
            device_id_type=MESH,
        )

    own_copies = [
        [
            [
                pltpu.make_async_copy(
                    ref.at[here(c), pl.ds(inner * block, block)],
                    cell(t, c, inner),
                    own_sem.at[t, c, inner],
                )
                for inner in range(owned)
            ]
            for c in range(chunks)
        ]
        for t, ref in enumerate((adj_hbm, dis_hbm))
    ]
    near_copies = [
        [
            remote(
                slab(t, c, 0), slab(t, c, 1), near_send.at[t, c], near_recv.at[t, c], partner, fr
            )
            for c in range(chunks)
        ]
        for t in range(2)
    ]
    relay_copies = [
        [
            remote(
                slab(t, c, 1), slab(t, c, 2), relay_send.at[t, c], relay_recv.at[t, c], target, fr
            )
            for c in range(chunks)
        ]
        for t in range(2)
    ]
    far_copies = [
        remote(far_out.at[c], far_in.at[c], far_send.at[c], far_recv.at[c], source, fr)
        for c in range(chunks)
    ]
    back_copies = [
        remote(near_out.at[c], near_in.at[c], back_send.at[c], back_recv.at[c], partner, fr)
        for c in range(chunks)
    ]
    peers = [(fr + d) % n_freq for d in range(n_freq)]
    pack_copies = [
        remote(pack.at[0], pack.at[d], pack_send.at[d], pack_recv.at[d], me, peers[d])
        for d in range(1, n_freq)
    ]
    pair = pair_of(n_freq)
    teams = n_freq // pair
    team = fr // pair
    rank = fr % pair
    other = (rank + 1) % pair
    first_copies = [
        remote(
            first_out.at[s, other],
            first_in.at[s],
            first_send.at[s],
            first_recv.at[s],
            me,
            team * pair + other,
        )
        for s in range(sub_here)
    ]
    away = [(team + d) % teams for d in range(teams)]
    second_copies = [
        [
            remote(
                second_out.at[s, d],
                second_in.at[s, d],
                second_send.at[s, d],
                second_recv.at[s, d],
                me,
                away[d] * pair + rank,
            )
            for d in range(1, teams)
        ]
        for s in range(sub_here)
    ]

    barrier = pltpu.get_barrier_semaphore()

    def greet(sub, freq):
        pl.semaphore_signal(barrier, inc=1, device_id=(sub, freq), device_id_type=MESH)

    greet(partner, fr)
    for d in range(1, n_freq):
        greet(me, peers[d])

    @pl.when(has_target)
    def _():
        greet(target, fr)

    @pl.when(has_source)
    def _():
        greet(source, fr)

    for copies in own_copies[0] + own_copies[1]:
        for copy in copies:
            copy.start()
    for copy in small_copies + weight_copies:
        copy.start()

    for ref in (*win_a, *win_d):
        ref[spare] = jnp.zeros(ref.shape[1:], ref.dtype)
    runs[n_slots] = jnp.zeros(runs.shape[1:], runs.dtype)
    flex_acc[...] = jnp.zeros_like(flex_acc)
    eig_acc[...] = jnp.zeros_like(eig_acc)

    with jax.named_scope("barrier"):
        pl.semaphore_wait(
            barrier, n_freq + has_target.astype(jnp.int32) + has_source.astype(jnp.int32)
        )
    def send(t):
        for c in range(chunks):
            for copy in own_copies[t][c]:
                copy.wait()
            near_copies[t][c].start()

    leads = rank == 0
    follows = rank != 0

    @pl.when(leads)
    def _():
        send(0)
        send(1)

    def relay(t, c):
        with jax.named_scope(f"relay{t}{c}"):
            near_copies[t][c].wait_recv()

            @pl.when(has_target)
            def _():
                relay_copies[t][c].start()

    def relayed(t, c):
        with jax.named_scope(f"relayed{t}{c}"):

            @pl.when(has_source)
            def _():
                relay_copies[t][c].wait_recv()

    with jax.named_scope("small"):
        for copy in small_copies:
            copy.wait()

    one, none = jnp.int32(1), jnp.int32(0)
    keys = []
    for s in range(sub_here):
        for k in range(slots):
            named = inc_ref[s, k]
            live = k < count_ref[s]
            key = jnp.int32(spare)
            for w, owner in enumerate((me, partner, me - 1 + 2 * odd)):
                for inner in range(owned):
                    hit = live & (named == owner * owned + inner)
                    key = jnp.where(hit, jnp.int32(w * owned + inner), key)
            block_tab[s * slots + k] = key
            keys.append(key)

    def count(tests):
        total = none
        for test in tests:
            total = total + jnp.where(test, one, none)
        return total

    ranks = [
        count(
            [keys[j] <= keys[i] for j in range(i)]
            + [keys[j] < keys[i] for j in range(i + 1, n_slots)]
        )
        for i in range(n_slots)
    ]
    before = None
    for r in range(n_slots):
        index, key = none, none
        for i in range(n_slots):
            chosen = ranks[i] == r
            index = jnp.where(chosen, jnp.int32(i), index)
            key = jnp.where(chosen, keys[i], key)
        order_tab[r] = index
        if r:
            keep_tab[r] = jnp.where(key == before, jnp.float32(1), jnp.float32(0))
        before = key
    for b in range(3 * owned):
        hits = count([key == b for key in keys])
        upto = count([key <= b for key in keys])
        last_tab[b] = jnp.where(hits > 0, upto - 1, jnp.int32(n_slots))

    if pair > 1:

        @pl.when(follows)
        def _():
            send(0)

    for c in range(chunks):
        relay(0, c)
        if c == chunks - 1 and pair > 1:

            @pl.when(follows)
            def _():
                send(1)

    def gather(ref, s, where):
        return jnp.concatenate(
            [ref[block_tab[s * slots + k], where, :] for k in range(slots)],
            axis=1,
        )

    def scales(c, s):
        w2 = freq_ref[c]
        w4 = w2 * w2
        inverse = 1.0 / (eig_ref[pl.ds(s, 1), :] - w2)
        mode_index = lax.broadcasted_iota(jnp.int32, (1, modes), 1)
        factor = jnp.where(mode_index < mode_ref[s], w4 * inverse, 0.0)
        return w2, w4, inverse, factor

    tile = 2 * block if slots % 2 == 0 else block

    def respond(p):
        firsts, weights = [], []
        for s in range(sub_here):
            a = gather(win_a[p], s, pl.ds(0, group * rows))
            ma = dot(a, coup[s], NT)
            parts = []
            for i in range(group):
                c = p * group + i
                factor = scales(c, s)[3]
                piece = ma[i * rows : (i + 1) * rows]
                modal[s, here(c), :] = piece
                parts.append((-factor * piece).astype(jnp.bfloat16))
            wa = jnp.concatenate(parts, axis=0)
            weight_a[s, pl.ds(p * group * rows, group * rows), :] = wa
            firsts.append(a)
            weights.append(wa)
        for s in range(sub_here):
            a, wa = firsts[s], weights[s]
            if s == min(1, sub_here - 1) and p == halves - 1:
                pass_on(2)
            for n in range(kb // tile):
                lanes = slice(n * tile, (n + 1) * tile)
                plain = dot(a, stiff[s, lanes, :], NT) + dot(wa, coup[s, :, lanes], NN)
                inert = dot(a, mass[s, lanes, :], NT)
                for i in range(group):
                    c = p * group + i
                    w2, w4 = scales(c, s)[:2]
                    span = slice(i * rows, (i + 1) * rows)
                    value = (
                        plain[span]
                        - w2 * inert[span]
                        - (w4 * flex_ref[s : s + 1, lanes]) * a[span, lanes].astype(jnp.float32)
                    )
                    for k in range(tile // block):
                        slot = s * slots + n * (tile // block) + k
                        resp[slot, within(c), :] = value[:, k * block : (k + 1) * block]

    def spread(c):
        with jax.named_scope(f"spread{c}"):
            total = None
            for r in range(n_slots):
                term = resp[order_tab[r], within(c), :]
                total = term if total is None else total * keep_tab[r] + term
                runs[r] = total
            for place in (2, 1, 0):
                for inner in range(owned):
                    value = runs[last_tab[place * owned + inner]]
                    lane = pl.ds(inner * block, block)
                    if place == 0:
                        out_ref[here(c), lane] = value
                    elif place == 1:
                        near_acc[c, :, lane] = value
                    else:
                        far_out[c, :, lane] = value.astype(far_out.dtype)
                if place == 2:

                    @pl.when(has_source)
                    def _():
                        far_copies[c].start()

            @pl.when(jnp.logical_not(has_target))
            def _():
                near_out[c] = near_acc[c].astype(near_out.dtype)
                back_copies[c].start()

    def plan(c, stages):
        return stages[c * len(stages) // chunks]

    def pass_on(position):
        lead = [c for c in range(chunks) if plan(c, (0, 0, 1, 1)) == position]
        follow = [c for c in range(chunks) if plan(c, (1, 2, 2, 3)) == position]
        if pair == 1 or lead == follow:
            for c in lead:
                relay(1, c)
            return

        @pl.when(leads)
        def _():
            for c in lead:
                relay(1, c)

        @pl.when(follows)
        def _():
            for c in follow:
                relay(1, c)

    pass_on(0)
    for p in range(halves):
        for i in range(group):
            relayed(0, p * group + i)
        if p == 0:
            with jax.named_scope("weights"):
                for copy in weight_copies:
                    copy.wait()
        with jax.named_scope(f"respond{p}"):
            respond(p)
        for i in range(group):
            spread(p * group + i)
        if p == 0:
            pass_on(1)
    pass_on(3)
    def modal_part(c):
        lefts, rights = [], []
        for s in range(sub_here):
            w2, w4, inverse, factor = scales(c, s)
            d = gather(win_d[c], s, pl.ds(0, rows))
            a = gather(win_a[c // group], s, within(c))
            md = dot(d, coup[s], NT)
            wd = (-factor * md).astype(jnp.bfloat16)
            eig_acc[s] += (factor * inverse) * fold(modal[s, here(c), :] * md)
            lefts.append(jnp.concatenate([weight_a[s, here(c), :], wd], axis=0))
            rights.append(jnp.concatenate([d, a], axis=0))
        for s in range(sub_here):
            value = dot(lefts[s], rights[s], TN)
            if c:
                value = value + grad[s]
            grad[s] = value
            if c + 1 == chunks and pair > 1:
                for j in range(n_freq):
                    first_out[s, j % pair, j // pair] = value[
                        :, j * part : (j + 1) * part
                    ].astype(first_out.dtype)
        if c + 1 == chunks and pair > 1:
            for copy in first_copies:
                copy.start()

    def flex_part(c):
        w4 = freq_ref[c] * freq_ref[c]
        for place in range(3):
            for inner in range(owned):
                b = place * owned + inner
                a = win_a[c // group][b, within(c), :].astype(jnp.float32)
                d = win_d[c][b].astype(jnp.float32)
                flex_acc[b] += -w4 * fold(a * d)

    def combine(c):
        with jax.named_scope(f"combine{c}"):

            @pl.when(has_target)
            def _():
                far_copies[c].wait_recv()
                near_out[c] = (near_acc[c] + far_in[c].astype(jnp.float32)).astype(
                    near_out.dtype
                )
                back_copies[c].start()

    def finish(c):
        with jax.named_scope(f"finish{c}"):
            back_copies[c].wait_recv()
            out_ref[here(c), :] += near_in[c].astype(jnp.float32)

    combined = 0
    for c in range(chunks):
        relayed(1, c)
        with jax.named_scope(f"modal{c}"):
            modal_part(c)
        with jax.named_scope(f"flex{c}"):
            flex_part(c)
        if c == chunks - 2:
            combine(combined)
            combined += 1

    with jax.named_scope("pack"):
        wide = max(block, modes)
        pack[0] = jnp.zeros(pack.shape[1:], pack.dtype)
        for s in range(sub_here):
            base = s * (slots + 1)
            for k in range(slots):
                pack[0, base + k : base + k + 1, 0:block] = jnp.sum(
                    flex_acc[block_tab[s * slots + k]], axis=0, keepdims=True
                )
            pack[0, base + slots : base + slots + 1, 0:modes] = jnp.sum(
                eig_acc[s], axis=0, keepdims=True
            )
        for copy in pack_copies:
            copy.start()

    while combined < chunks:
        combine(combined)
        combined += 1

    for s in range(sub_here):
        with jax.named_scope(f"second{s}"):
            if pair > 1:
                first_copies[s].wait_recv()
            for d in range(1, teams):
                j = away[d]
                lane = pl.ds(pl.multiple_of((j * pair + rank) * part, part), part)
                value = grad[s, :, lane]
                if pair > 1:
                    value = value + first_in[s, j].astype(jnp.float32)
                second_out[s, d] = value.astype(second_out.dtype)
            for copy in second_copies[s]:
                copy.start()

    for c in range(chunks):
        finish(c)

    with jax.named_scope("packwait"):
        for copy in pack_copies:
            copy.wait_recv()
    total = None
    for i in range(n_freq):
        term = pack[(fr - i + n_freq) % n_freq]
        total = term if total is None else total + term
    for s in range(sub_here):
        base = s * (slots + 1)
        for k in range(slots):
            flex_out[s : s + 1, k * block : (k + 1) * block] = total[
                base + k : base + k + 1, 0:block
            ]
        eig_out[s : s + 1, :] = total[base + slots : base + slots + 1, 0:modes]
    for s in range(sub_here):
        with jax.named_scope(f"grad{s}"):
            lane = pl.ds(pl.multiple_of(fr * part, part), part)
            value = grad[s, :, lane]
            if pair > 1:
                value = value + first_in[s, team].astype(jnp.float32)
            for d in range(1, teams):
                second_copies[s][d - 1].wait_recv()
                value = value + second_in[s, d].astype(jnp.float32)
            cg_out_ref[s] = value

    with jax.named_scope("end"):
        for c in range(chunks):
            for t in range(2):
                near_copies[t][c].wait_send()
            back_copies[c].wait_send()

        @pl.when(has_target)
        def _():
            for c in range(chunks):
                for t in range(2):
                    relay_copies[t][c].wait_send()

        @pl.when(has_source)
        def _():
            for c in range(chunks):
                far_copies[c].wait_send()

        for copy in pack_copies:
            copy.wait_send()
        for s in range(sub_here):
            if pair > 1:
                first_copies[s].wait_send()
            for copy in second_copies[s]:
                copy.wait_send()


def write_out(*refs):
    count = len(refs) // 2
    sems = refs[-1]
    copies = [
        pltpu.make_async_copy(refs[i], refs[count + i], sems.at[i]) for i in range(count)
    ]
    for copy in copies:
        copy.start()
    for copy in copies:
        copy.wait()


def shards(
    n_sub,
    n_freq,
    freq_squared,
    displacement,
    adjoint,
    incidence,
    block_count,
    mode_count,
    stiffness,
    mass_matrix,
    coupling,
    eigenvalues,
    flexibility,
):
    sub_here, slots = incidence.shape
    columns, owned_cells = displacement.shape
    chunks = freq_squared.shape[0]
    rows = columns // chunks
    kb = stiffness.shape[1]
    block = kb // slots
    owned = owned_cells // block
    modes = coupling.shape[1]
    part = kb // n_freq
    group = group_of(chunks)
    pair = pair_of(n_freq)
    teams = n_freq // pair
    n_slots = sub_here * slots
    pack_rows = -(-(sub_here * (slots + 1)) // 8) * 8
    bf16, f32, i32 = jnp.bfloat16, jnp.float32, jnp.int32
    vmem = pl.BlockSpec(memory_space=pltpu.VMEM)
    hbm = pl.BlockSpec(memory_space=pltpu.HBM)
    dma = pltpu.SemaphoreType.DMA
    slab = (chunks, rows, owned_cells)
    scratch = (
        [
            pltpu.VMEM((3 * owned + 1, group * rows, block), bf16)
            for _ in range(chunks // group)
        ]
        + [pltpu.VMEM((3 * owned + 1, rows, block), bf16) for _ in range(chunks)]
        + [
            pltpu.SMEM(freq_squared.shape, f32),
            pltpu.SMEM(incidence.shape, i32),
            pltpu.SMEM(block_count.shape, i32),
            pltpu.SMEM(mode_count.shape, i32),
            pltpu.SMEM((n_slots,), i32),
            pltpu.SMEM((n_slots,), i32),
            pltpu.SMEM((3 * owned,), i32),
            pltpu.SMEM((n_slots,), f32),
            pltpu.VMEM(eigenvalues.shape, f32),
            pltpu.VMEM(flexibility.shape, f32),
            pltpu.VMEM(stiffness.shape, bf16),
            pltpu.VMEM(mass_matrix.shape, bf16),
            pltpu.VMEM(coupling.shape, bf16),
            pltpu.VMEM((n_slots, group * rows, block), f32),
            pltpu.VMEM((n_slots + 1, rows, block), f32),
            pltpu.VMEM((sub_here, columns, modes), f32),
            pltpu.VMEM((sub_here, columns, modes), bf16),
            pltpu.VMEM(slab, f32),
            pltpu.VMEM(slab, bf16),
            pltpu.VMEM(slab, bf16),
            pltpu.VMEM(slab, bf16),
            pltpu.VMEM(slab, bf16),
            pltpu.VMEM((3 * owned + 1, 8, block), f32),
            pltpu.VMEM((sub_here, 8, modes), f32),
            pltpu.VMEM((n_freq, pack_rows, max(block, modes)), f32),
            pltpu.VMEM((sub_here, modes, kb), f32),
            pltpu.VMEM((sub_here, pair, teams, modes, part), bf16),
            pltpu.VMEM((sub_here, teams, modes, part), bf16),
            pltpu.VMEM((sub_here, teams, modes, part), bf16),
            pltpu.VMEM((sub_here, teams, modes, part), bf16),
            dma((2, chunks, owned)),
            dma((3,)),
            dma((6,)),
            dma((2, chunks)),
            dma((2, chunks)),
            dma((2, chunks)),
            dma((2, chunks)),
            dma((chunks,)),
            dma((chunks,)),
            dma((chunks,)),
            dma((chunks,)),
            dma((n_freq,)),
            dma((n_freq,)),
            dma((sub_here,)),
            dma((sub_here,)),
            dma((sub_here, teams)),
            dma((sub_here, teams)),
        ]
    )
    results = pl.pallas_call(
        functools.partial(kernel, n_sub, n_freq, chunks),
        out_shape=(
            jax.ShapeDtypeStruct((columns, owned_cells), f32),
            jax.ShapeDtypeStruct((sub_here, modes), f32),
            jax.ShapeDtypeStruct((sub_here, modes, part), f32),
            jax.ShapeDtypeStruct((sub_here, kb), f32),
        ),
        in_specs=[hbm] * 11,
        out_specs=(vmem,) * 4,
        scratch_shapes=scratch,
        compiler_params=pltpu.CompilerParams(
            collective_id=0, has_side_effects=True, vmem_limit_bytes=48 * 1024 * 1024
        ),
    )(
        *(
            pltpu.with_memory_space_constraint(x, pltpu.HBM)
            for x in (
                freq_squared,
                incidence,
                block_count,
                mode_count,
                eigenvalues,
                flexibility,
                adjoint,
                displacement,
                stiffness,
                mass_matrix,
                coupling,
            )
        )
    )
    return pl.pallas_call(
        write_out,
        out_shape=tuple(jax.ShapeDtypeStruct(x.shape, x.dtype) for x in results),
        in_specs=[vmem] * 4,
        out_specs=(pl.BlockSpec(memory_space=pltpu.HBM),) * 4,
        scratch_shapes=[dma((4,))],
        compiler_params=pltpu.CompilerParams(vmem_limit_bytes=4 * 1024 * 1024),
    )(*results)


def solution(mesh):
    in_specs = (
        P("freq"),
        P("freq", "sub"),
        P("freq", "sub"),
        P("sub", None),
        P("sub"),
        P("sub"),
        P("sub", None, None),
        P("sub", None, None),
        P("sub", None, None),
        P("sub", None),
        P("sub", None),
    )
    out_specs = (P("freq", "sub"), P("sub", None), P("sub", None, "freq"), P("sub", None))
    body = functools.partial(shards, mesh.shape["sub"], mesh.shape["freq"])
    return jax.shard_map(body, mesh=mesh, in_specs=in_specs, out_specs=out_specs, check_vma=False)
```

```python
import functools

import jax
import jax.numpy as jnp
from jax import lax
from jax.experimental import pallas as pl
from jax.experimental.pallas import tpu as pltpu
from jax.sharding import PartitionSpec as P

MESH = pl.DeviceIdType.MESH
NT = (((1,), (1,)), ((), ()))
NN = (((1,), (0,)), ((), ()))
TN = (((0,), (0,)), ((), ()))


def dot(a, b, dims):
    return lax.dot_general(a, b, dims, preferred_element_type=jnp.float32)


def group_of(chunks):
    return 2 if chunks % 2 == 0 else 1


def pair_of(n_freq):
    return 2 if n_freq % 2 == 0 else 1


def fold(x):
    return jnp.sum(x.reshape(x.shape[0] // 8, 8, x.shape[1]), axis=0)


def kernel(
    n_sub,
    n_freq,
    chunks,
    freq_hbm,
    inc_hbm,
    count_hbm,
    mode_hbm,
    eig_hbm,
    flex_hbm,
    adj_hbm,
    dis_hbm,
    stiff_hbm,
    mass_hbm,
    coup_hbm,
    out_ref,
    eig_out,
    cg_out_ref,
    flex_out,
    *scratch,
):
    group = group_of(chunks)
    halves = chunks // group
    win_a = scratch[:halves]
    win_d = scratch[halves : halves + chunks]
    (
        freq_ref,
        inc_ref,
        count_ref,
        mode_ref,
        block_tab,
        order_tab,
        last_tab,
        keep_tab,
        eig_ref,
        flex_ref,
        stiff,
        mass,
        coup,
        resp,
        runs,
        modal,
        weight_a,
        near_acc,
        far_out,
        far_in,
        near_out,
        near_in,
        flex_acc,
        eig_acc,
        pack,
        grad,
        first_out,
        first_in,
        second_out,
        second_in,
        own_sem,
        weight_sem,
        small_sem,
        near_send,
        near_recv,
        relay_send,
        relay_recv,
        far_send,
        far_recv,
        back_send,
        back_recv,
        pack_send,
        pack_recv,
        first_send,
        first_recv,
        second_send,
        second_recv,
    ) = scratch[halves + chunks :]
    sub_here, slots = inc_ref.shape
    columns, owned_cells = adj_hbm.shape
    rows = columns // chunks
    kb = stiff.shape[1]
    block = kb // slots
    owned = owned_cells // block
    modes = coup.shape[1]
    part = kb // n_freq
    n_slots = sub_here * slots
    spare = 3 * owned

    me = lax.axis_index("sub")
    fr = lax.axis_index("freq")
    odd = me % 2
    step = 2 - 4 * odd
    partner = me + 1 - 2 * odd
    target = me + step
    source = me - step
    has_target = (target >= 0) & (target < n_sub)
    has_source = (source >= 0) & (source < n_sub)
    target = jnp.clip(target, 0, n_sub - 1)
    source = jnp.clip(source, 0, n_sub - 1)

    weight_copies = [
        pltpu.make_async_copy(hbm, vmem, weight_sem.at[i])
        for i, (hbm, vmem) in enumerate(((coup_hbm, coup), (stiff_hbm, stiff), (mass_hbm, mass)))
    ]
    small_copies = [
        pltpu.make_async_copy(hbm, local, small_sem.at[i])
        for i, (hbm, local) in enumerate(
            (
                (freq_hbm, freq_ref),
                (inc_hbm, inc_ref),
                (count_hbm, count_ref),
                (mode_hbm, mode_ref),
                (eig_hbm, eig_ref),
                (flex_hbm, flex_ref),
            )
        )
    ]

    def here(c):
        return pl.ds(c * rows, rows)

    def within(c):
        return pl.ds((c % group) * rows, rows)

    def slab(t, c, place):
        blocks = pl.ds(place * owned, owned)
        if t == 0:
            return win_a[c // group].at[blocks, within(c), :]
        return win_d[c].at[blocks]

    def cell(t, c, inner):
        if t == 0:
            return win_a[c // group].at[inner, within(c), :]
        return win_d[c].at[inner]

    def remote(src, dst, send, recv, sub, freq):
        return pltpu.make_async_remote_copy(
            src_ref=src,
            dst_ref=dst,
            send_sem=send,
            recv_sem=recv,
            device_id=(sub, freq),
            device_id_type=MESH,
        )

    own_copies = [
        [
            [
                pltpu.make_async_copy(
                    ref.at[here(c), pl.ds(inner * block, block)],
                    cell(t, c, inner),
                    own_sem.at[t, c, inner],
                )
                for inner in range(owned)
            ]
            for c in range(chunks)
        ]
        for t, ref in enumerate((adj_hbm, dis_hbm))
    ]
    near_copies = [
        [
            remote(
                slab(t, c, 0), slab(t, c, 1), near_send.at[t, c], near_recv.at[t, c], partner, fr
            )
            for c in range(chunks)
        ]
        for t in range(2)
    ]
    relay_copies = [
        [
            remote(
                slab(t, c, 1), slab(t, c, 2), relay_send.at[t, c], relay_recv.at[t, c], target, fr
            )
            for c in range(chunks)
        ]
        for t in range(2)
    ]
    far_copies = [
        remote(far_out.at[c], far_in.at[c], far_send.at[c], far_recv.at[c], source, fr)
        for c in range(chunks)
    ]
    back_copies = [
        remote(near_out.at[c], near_in.at[c], back_send.at[c], back_recv.at[c], partner, fr)
        for c in range(chunks)
    ]
    peers = [(fr + d) % n_freq for d in range(n_freq)]
    pack_copies = [
        remote(pack.at[0], pack.at[d], pack_send.at[d], pack_recv.at[d], me, peers[d])
        for d in range(1, n_freq)
    ]
    pair = pair_of(n_freq)
    teams = n_freq // pair
    team = fr // pair
    rank = fr % pair
    other = (rank + 1) % pair
    first_copies = [
        remote(
            first_out.at[s, other],
            first_in.at[s],
            first_send.at[s],
            first_recv.at[s],
            me,
            team * pair + other,
        )
        for s in range(sub_here)
    ]
    away = [(team + d) % teams for d in range(teams)]
    second_copies = [
        [
            remote(
                second_out.at[s, d],
                second_in.at[s, d],
                second_send.at[s, d],
                second_recv.at[s, d],
                me,
                away[d] * pair + rank,
            )
            for d in range(1, teams)
        ]
        for s in range(sub_here)
    ]

    barrier = pltpu.get_barrier_semaphore()

    def greet(sub, freq):
        pl.semaphore_signal(barrier, inc=1, device_id=(sub, freq), device_id_type=MESH)

    greet(partner, fr)
    for d in range(1, n_freq):
        greet(me, peers[d])

    @pl.when(has_target)
    def _():
        greet(target, fr)

    @pl.when(has_source)
    def _():
        greet(source, fr)

    for copies in own_copies[0] + own_copies[1]:
        for copy in copies:
            copy.start()
    for copy in small_copies + weight_copies:
        copy.start()

    for ref in (*win_a, *win_d):
        ref[spare] = jnp.zeros(ref.shape[1:], ref.dtype)
    runs[n_slots] = jnp.zeros(runs.shape[1:], runs.dtype)
    flex_acc[...] = jnp.zeros_like(flex_acc)
    eig_acc[...] = jnp.zeros_like(eig_acc)

    with jax.named_scope("barrier"):
        pl.semaphore_wait(
            barrier, n_freq + has_target.astype(jnp.int32) + has_source.astype(jnp.int32)
        )
    def send(t):
        for c in range(chunks):
            for copy in own_copies[t][c]:
                copy.wait()
            near_copies[t][c].start()

    leads = rank == 0
    follows = rank != 0

    @pl.when(leads)
    def _():
        send(0)
        send(1)

    def relay(t, c):
        with jax.named_scope(f"relay{t}{c}"):
            near_copies[t][c].wait_recv()

            @pl.when(has_target)
            def _():
                relay_copies[t][c].start()

    def relayed(t, c):
        with jax.named_scope(f"relayed{t}{c}"):

            @pl.when(has_source)
            def _():
                relay_copies[t][c].wait_recv()

    with jax.named_scope("small"):
        for copy in small_copies:
            copy.wait()

    one, none = jnp.int32(1), jnp.int32(0)
    keys = []
    for s in range(sub_here):
        for k in range(slots):
            named = inc_ref[s, k]
            live = k < count_ref[s]
            key = jnp.int32(spare)
            for w, owner in enumerate((me, partner, me - 1 + 2 * odd)):
                for inner in range(owned):
                    hit = live & (named == owner * owned + inner)
                    key = jnp.where(hit, jnp.int32(w * owned + inner), key)
            block_tab[s * slots + k] = key
            keys.append(key)

    def count(tests):
        total = none
        for test in tests:
            total = total + jnp.where(test, one, none)
        return total

    ranks = [
        count(
            [keys[j] <= keys[i] for j in range(i)]
            + [keys[j] < keys[i] for j in range(i + 1, n_slots)]
        )
        for i in range(n_slots)
    ]
    before = None
    for r in range(n_slots):
        index, key = none, none
        for i in range(n_slots):
            chosen = ranks[i] == r
            index = jnp.where(chosen, jnp.int32(i), index)
            key = jnp.where(chosen, keys[i], key)
        order_tab[r] = index
        if r:
            keep_tab[r] = jnp.where(key == before, jnp.float32(1), jnp.float32(0))
        before = key
    for b in range(3 * owned):
        hits = count([key == b for key in keys])
        upto = count([key <= b for key in keys])
        last_tab[b] = jnp.where(hits > 0, upto - 1, jnp.int32(n_slots))

    if pair > 1:

        @pl.when(follows)
        def _():
            send(0)

    for c in range(chunks):
        relay(0, c)
        if c == chunks - 1 and pair > 1:

            @pl.when(follows)
            def _():
                send(1)

    def gather(ref, s, where):
        return jnp.concatenate(
            [ref[block_tab[s * slots + k], where, :] for k in range(slots)],
            axis=1,
        )

    def scales(c, s):
        w2 = freq_ref[c]
        w4 = w2 * w2
        inverse = 1.0 / (eig_ref[pl.ds(s, 1), :] - w2)
        mode_index = lax.broadcasted_iota(jnp.int32, (1, modes), 1)
        factor = jnp.where(mode_index < mode_ref[s], w4 * inverse, 0.0)
        return w2, w4, inverse, factor

    tile = 2 * block if slots % 2 == 0 else block

    def respond(p):
        firsts, weights = [], []
        for s in range(sub_here):
            a = gather(win_a[p], s, pl.ds(0, group * rows))
            ma = dot(a, coup[s], NT)
            parts = []
            for i in range(group):
                c = p * group + i
                factor = scales(c, s)[3]
                piece = ma[i * rows : (i + 1) * rows]
                modal[s, here(c), :] = piece
                parts.append((-factor * piece).astype(jnp.bfloat16))
            wa = jnp.concatenate(parts, axis=0)
            weight_a[s, pl.ds(p * group * rows, group * rows), :] = wa
            firsts.append(a)
            weights.append(wa)
        for s in range(sub_here):
            a, wa = firsts[s], weights[s]
            if s == min(1, sub_here - 1) and p == halves - 1:
                pass_on(2)
            for n in range(kb // tile):
                lanes = slice(n * tile, (n + 1) * tile)
                plain = dot(a, stiff[s, lanes, :], NT) + dot(wa, coup[s, :, lanes], NN)
                inert = dot(a, mass[s, lanes, :], NT)
                for i in range(group):
                    c = p * group + i
                    w2, w4 = scales(c, s)[:2]
                    span = slice(i * rows, (i + 1) * rows)
                    value = (
                        plain[span]
                        - w2 * inert[span]
                        - (w4 * flex_ref[s : s + 1, lanes]) * a[span, lanes].astype(jnp.float32)
                    )
                    for k in range(tile // block):
                        slot = s * slots + n * (tile // block) + k
                        resp[slot, within(c), :] = value[:, k * block : (k + 1) * block]

    def spread(c):
        with jax.named_scope(f"spread{c}"):
            total = None
            for r in range(n_slots):
                term = resp[order_tab[r], within(c), :]
                total = term if total is None else total * keep_tab[r] + term
                runs[r] = total
            for place in (2, 1, 0):
                for inner in range(owned):
                    value = runs[last_tab[place * owned + inner]]
                    lane = pl.ds(inner * block, block)
                    if place == 0:
                        out_ref[here(c), lane] = value
                    elif place == 1:
                        near_acc[c, :, lane] = value
                    else:
                        far_out[c, :, lane] = value.astype(far_out.dtype)
                if place == 2:

                    @pl.when(has_source)
                    def _():
                        far_copies[c].start()

            @pl.when(jnp.logical_not(has_target))
            def _():
                near_out[c] = near_acc[c].astype(near_out.dtype)
                back_copies[c].start()

    def plan(c, stages):
        return stages[c * len(stages) // chunks]

    def pass_on(position):
        lead = [c for c in range(chunks) if plan(c, (0, 0, 1, 1)) == position]
        follow = [c for c in range(chunks) if plan(c, (1, 2, 2, 3)) == position]
        if pair == 1 or lead == follow:
            for c in lead:
                relay(1, c)
            return

        @pl.when(leads)
        def _():
            for c in lead:
                relay(1, c)

        @pl.when(follows)
        def _():
            for c in follow:
                relay(1, c)

    pass_on(0)
    for p in range(halves):
        for i in range(group):
            relayed(0, p * group + i)
        if p == 0:
            with jax.named_scope("weights"):
                for copy in weight_copies:
                    copy.wait()
        with jax.named_scope(f"respond{p}"):
            respond(p)
        for i in range(group):
            spread(p * group + i)
        if p == 0:
            pass_on(1)
    pass_on(3)

    def modal_part(c):
        lefts, rights = [], []
        for s in range(sub_here):
            w2, w4, inverse, factor = scales(c, s)
            d = gather(win_d[c], s, pl.ds(0, rows))
            a = gather(win_a[c // group], s, within(c))
            md = dot(d, coup[s], NT)
            wd = (-factor * md).astype(jnp.bfloat16)
            eig_acc[s] += (factor * inverse) * fold(modal[s, here(c), :] * md)
            lefts.append(jnp.concatenate([weight_a[s, here(c), :], wd], axis=0))
            rights.append(jnp.concatenate([d, a], axis=0))
        for s in range(sub_here):
            value = dot(lefts[s], rights[s], TN)
            if c:
                value = value + grad[s]
            grad[s] = value
            if c + 1 == chunks and pair > 1:
                for j in range(n_freq):
                    first_out[s, j % pair, j // pair] = value[
                        :, j * part : (j + 1) * part
                    ].astype(first_out.dtype)
        if c + 1 == chunks and pair > 1:
            for copy in first_copies:
                copy.start()

    def flex_part(c):
        w4 = freq_ref[c] * freq_ref[c]
        for place in range(3):
            for inner in range(owned):
                b = place * owned + inner
                a = win_a[c // group][b, within(c), :].astype(jnp.float32)
                d = win_d[c][b].astype(jnp.float32)
                flex_acc[b] += -w4 * fold(a * d)

    def combine(c, when=True):
        with jax.named_scope(f"combine{c}"):

            @pl.when(has_target & when)
            def _():
                far_copies[c].wait_recv()
                near_out[c] = (near_acc[c] + far_in[c].astype(jnp.float32)).astype(
                    near_out.dtype
                )
                back_copies[c].start()

    def finish(c):
        with jax.named_scope(f"finish{c}"):
            back_copies[c].wait_recv()
            out_ref[here(c), :] += near_in[c].astype(jnp.float32)

    combined = 0
    for c in range(chunks):
        relayed(1, c)
        with jax.named_scope(f"modal{c}"):
            modal_part(c)
        with jax.named_scope(f"flex{c}"):
            flex_part(c)
        if c == min(group, chunks) - 1:
            for i in range(group):
                combine(i, odd == 1)
            combined = group
        if c == chunks - 2:
            combine(0, odd == 0)
    for i in range(1 if chunks > 1 else 0, group):
        combine(i, odd == 0)

    with jax.named_scope("pack"):
        wide = max(block, modes)
        pack[0] = jnp.zeros(pack.shape[1:], pack.dtype)
        for s in range(sub_here):
            base = s * (slots + 1)
            for k in range(slots):
                pack[0, base + k : base + k + 1, 0:block] = jnp.sum(
                    flex_acc[block_tab[s * slots + k]], axis=0, keepdims=True
                )
            pack[0, base + slots : base + slots + 1, 0:modes] = jnp.sum(
                eig_acc[s], axis=0, keepdims=True
            )
        for copy in pack_copies:
            copy.start()

    for c in range(combined, chunks - 1):
        combine(c, odd == 1)

    for s in range(sub_here):
        with jax.named_scope(f"second{s}"):
            if pair > 1:
                first_copies[s].wait_recv()
            for d in range(1, teams):
                j = away[d]
                lane = pl.ds(pl.multiple_of((j * pair + rank) * part, part), part)
                value = grad[s, :, lane]
                if pair > 1:
                    value = value + first_in[s, j].astype(jnp.float32)
                second_out[s, d] = value.astype(second_out.dtype)
            for copy in second_copies[s]:
                copy.start()

    for c in range(combined, chunks - 1):
        combine(c, odd == 0)
    for c in range(max(combined, chunks - 1), chunks):
        combine(c)

    for c in range(chunks):
        finish(c)

    with jax.named_scope("packwait"):
        for copy in pack_copies:
            copy.wait_recv()
    total = None
    for i in range(n_freq):
        term = pack[(fr - i + n_freq) % n_freq]
        total = term if total is None else total + term
    for s in range(sub_here):
        base = s * (slots + 1)
        for k in range(slots):
            flex_out[s : s + 1, k * block : (k + 1) * block] = total[
                base + k : base + k + 1, 0:block
            ]
        eig_out[s : s + 1, :] = total[base + slots : base + slots + 1, 0:modes]
    for s in range(sub_here):
        with jax.named_scope(f"grad{s}"):
            lane = pl.ds(pl.multiple_of(fr * part, part), part)
            value = grad[s, :, lane]
            if pair > 1:
                value = value + first_in[s, team].astype(jnp.float32)
            for d in range(1, teams):
                second_copies[s][d - 1].wait_recv()
                value = value + second_in[s, d].astype(jnp.float32)
            cg_out_ref[s] = value

    with jax.named_scope("end"):
        for c in range(chunks):
            for t in range(2):
                near_copies[t][c].wait_send()
            back_copies[c].wait_send()

        @pl.when(has_target)
        def _():
            for c in range(chunks):
                for t in range(2):
                    relay_copies[t][c].wait_send()

        @pl.when(has_source)
        def _():
            for c in range(chunks):
                far_copies[c].wait_send()

        for copy in pack_copies:
            copy.wait_send()
        for s in range(sub_here):
            if pair > 1:
                first_copies[s].wait_send()
            for copy in second_copies[s]:
                copy.wait_send()


def write_out(*refs):
    count = len(refs) // 2
    sems = refs[-1]
    copies = [
        pltpu.make_async_copy(refs[i], refs[count + i], sems.at[i]) for i in range(count)
    ]
    for copy in copies:
        copy.start()
    for copy in copies:
        copy.wait()


def shards(
    n_sub,
    n_freq,
    freq_squared,
    displacement,
    adjoint,
    incidence,
    block_count,
    mode_count,
    stiffness,
    mass_matrix,
    coupling,
    eigenvalues,
    flexibility,
):
    sub_here, slots = incidence.shape
    columns, owned_cells = displacement.shape
    chunks = freq_squared.shape[0]
    rows = columns // chunks
    kb = stiffness.shape[1]
    block = kb // slots
    owned = owned_cells // block
    modes = coupling.shape[1]
    part = kb // n_freq
    group = group_of(chunks)
    pair = pair_of(n_freq)
    teams = n_freq // pair
    n_slots = sub_here * slots
    pack_rows = -(-(sub_here * (slots + 1)) // 8) * 8
    bf16, f32, i32 = jnp.bfloat16, jnp.float32, jnp.int32
    vmem = pl.BlockSpec(memory_space=pltpu.VMEM)
    hbm = pl.BlockSpec(memory_space=pltpu.HBM)
    dma = pltpu.SemaphoreType.DMA
    slab = (chunks, rows, owned_cells)
    scratch = (
        [
            pltpu.VMEM((3 * owned + 1, group * rows, block), bf16)
            for _ in range(chunks // group)
        ]
        + [pltpu.VMEM((3 * owned + 1, rows, block), bf16) for _ in range(chunks)]
        + [
            pltpu.SMEM(freq_squared.shape, f32),
            pltpu.SMEM(incidence.shape, i32),
            pltpu.SMEM(block_count.shape, i32),
            pltpu.SMEM(mode_count.shape, i32),
            pltpu.SMEM((n_slots,), i32),
            pltpu.SMEM((n_slots,), i32),
            pltpu.SMEM((3 * owned,), i32),
            pltpu.SMEM((n_slots,), f32),
            pltpu.VMEM(eigenvalues.shape, f32),
            pltpu.VMEM(flexibility.shape, f32),
            pltpu.VMEM(stiffness.shape, bf16),
            pltpu.VMEM(mass_matrix.shape, bf16),
            pltpu.VMEM(coupling.shape, bf16),
            pltpu.VMEM((n_slots, group * rows, block), f32),
            pltpu.VMEM((n_slots + 1, rows, block), f32),
            pltpu.VMEM((sub_here, columns, modes), f32),
            pltpu.VMEM((sub_here, columns, modes), bf16),
            pltpu.VMEM(slab, f32),
            pltpu.VMEM(slab, bf16),
            pltpu.VMEM(slab, bf16),
            pltpu.VMEM(slab, bf16),
            pltpu.VMEM(slab, bf16),
            pltpu.VMEM((3 * owned + 1, 8, block), f32),
            pltpu.VMEM((sub_here, 8, modes), f32),
            pltpu.VMEM((n_freq, pack_rows, max(block, modes)), f32),
            pltpu.VMEM((sub_here, modes, kb), f32),
            pltpu.VMEM((sub_here, pair, teams, modes, part), bf16),
            pltpu.VMEM((sub_here, teams, modes, part), bf16),
            pltpu.VMEM((sub_here, teams, modes, part), bf16),
            pltpu.VMEM((sub_here, teams, modes, part), bf16),
            dma((2, chunks, owned)),
            dma((3,)),
            dma((6,)),
            dma((2, chunks)),
            dma((2, chunks)),
            dma((2, chunks)),
            dma((2, chunks)),
            dma((chunks,)),
            dma((chunks,)),
            dma((chunks,)),
            dma((chunks,)),
            dma((n_freq,)),
            dma((n_freq,)),
            dma((sub_here,)),
            dma((sub_here,)),
            dma((sub_here, teams)),
            dma((sub_here, teams)),
        ]
    )
    results = pl.pallas_call(
        functools.partial(kernel, n_sub, n_freq, chunks),
        out_shape=(
            jax.ShapeDtypeStruct((columns, owned_cells), f32),
            jax.ShapeDtypeStruct((sub_here, modes), f32),
            jax.ShapeDtypeStruct((sub_here, modes, part), f32),
            jax.ShapeDtypeStruct((sub_here, kb), f32),
        ),
        in_specs=[hbm] * 11,
        out_specs=(vmem,) * 4,
        scratch_shapes=scratch,
        compiler_params=pltpu.CompilerParams(
            collective_id=0, has_side_effects=True, vmem_limit_bytes=48 * 1024 * 1024
        ),
    )(
        *(
            pltpu.with_memory_space_constraint(x, pltpu.HBM)
            for x in (
                freq_squared,
                incidence,
                block_count,
                mode_count,
                eigenvalues,
                flexibility,
                adjoint,
                displacement,
                stiffness,
                mass_matrix,
                coupling,
            )
        )
    )
    return pl.pallas_call(
        write_out,
        out_shape=tuple(jax.ShapeDtypeStruct(x.shape, x.dtype) for x in results),
        in_specs=[vmem] * 4,
        out_specs=(pl.BlockSpec(memory_space=pltpu.HBM),) * 4,
        scratch_shapes=[dma((4,))],
        compiler_params=pltpu.CompilerParams(vmem_limit_bytes=4 * 1024 * 1024),
    )(*results)


def solution(mesh):
    in_specs = (
        P("freq"),
        P("freq", "sub"),
        P("freq", "sub"),
        P("sub", None),
        P("sub"),
        P("sub"),
        P("sub", None, None),
        P("sub", None, None),
        P("sub", None, None),
        P("sub", None),
        P("sub", None),
    )
    out_specs = (P("freq", "sub"), P("sub", None), P("sub", None, "freq"), P("sub", None))
    body = functools.partial(shards, mesh.shape["sub"], mesh.shape["freq"])
    return jax.shard_map(body, mesh=mesh, in_specs=in_specs, out_specs=out_specs, check_vma=False)
```

```python
import functools

import jax
import jax.numpy as jnp
from jax import lax
from jax.experimental import pallas as pl
from jax.experimental.pallas import tpu as pltpu
from jax.sharding import PartitionSpec as P

MESH = pl.DeviceIdType.MESH
NT = (((1,), (1,)), ((), ()))
NN = (((1,), (0,)), ((), ()))
TN = (((0,), (0,)), ((), ()))


def dot(a, b, dims):
    return lax.dot_general(a, b, dims, preferred_element_type=jnp.float32)


def group_of(chunks):
    return 2 if chunks % 2 == 0 else 1


def pair_of(n_freq):
    return 2 if n_freq % 2 == 0 else 1


def fold(x):
    return jnp.sum(x.reshape(x.shape[0] // 8, 8, x.shape[1]), axis=0)


def kernel(
    n_sub,
    n_freq,
    chunks,
    freq_hbm,
    inc_hbm,
    count_hbm,
    mode_hbm,
    eig_hbm,
    flex_hbm,
    adj_hbm,
    dis_hbm,
    stiff_hbm,
    mass_hbm,
    coup_hbm,
    out_ref,
    eig_out,
    cg_out_ref,
    flex_out,
    *scratch,
):
    group = group_of(chunks)
    halves = chunks // group
    win_a = scratch[:halves]
    win_d = scratch[halves : halves + chunks]
    (
        freq_ref,
        inc_ref,
        count_ref,
        mode_ref,
        block_tab,
        order_tab,
        last_tab,
        keep_tab,
        eig_ref,
        flex_ref,
        stiff,
        mass,
        coup,
        resp,
        runs,
        modal,
        weight_a,
        near_acc,
        far_out,
        far_in,
        near_out,
        near_in,
        flex_acc,
        eig_acc,
        pack,
        grad,
        first_out,
        first_in,
        second_out,
        second_in,
        own_sem,
        weight_sem,
        small_sem,
        near_send,
        near_recv,
        relay_send,
        relay_recv,
        far_send,
        far_recv,
        back_send,
        back_recv,
        pack_send,
        pack_recv,
        first_send,
        first_recv,
        second_send,
        second_recv,
    ) = scratch[halves + chunks :]
    sub_here, slots = inc_ref.shape
    columns, owned_cells = adj_hbm.shape
    rows = columns // chunks
    kb = stiff.shape[1]
    block = kb // slots
    owned = owned_cells // block
    modes = coup.shape[1]
    part = kb // n_freq
    n_slots = sub_here * slots
    spare = 3 * owned

    me = lax.axis_index("sub")
    fr = lax.axis_index("freq")
    odd = me % 2
    step = 2 - 4 * odd
    partner = me + 1 - 2 * odd
    target = me + step
    source = me - step
    has_target = (target >= 0) & (target < n_sub)
    has_source = (source >= 0) & (source < n_sub)
    target = jnp.clip(target, 0, n_sub - 1)
    source = jnp.clip(source, 0, n_sub - 1)

    weight_copies = [
        pltpu.make_async_copy(hbm, vmem, weight_sem.at[i])
        for i, (hbm, vmem) in enumerate(((coup_hbm, coup), (stiff_hbm, stiff), (mass_hbm, mass)))
    ]
    small_copies = [
        pltpu.make_async_copy(hbm, local, small_sem.at[i])
        for i, (hbm, local) in enumerate(
            (
                (freq_hbm, freq_ref),
                (inc_hbm, inc_ref),
                (count_hbm, count_ref),
                (mode_hbm, mode_ref),
                (eig_hbm, eig_ref),
                (flex_hbm, flex_ref),
            )
        )
    ]

    def here(c):
        return pl.ds(c * rows, rows)

    def within(c):
        return pl.ds((c % group) * rows, rows)

    def slab(t, c, place):
        blocks = pl.ds(place * owned, owned)
        if t == 0:
            return win_a[c // group].at[blocks, within(c), :]
        return win_d[c].at[blocks]

    def lot(t, c):
        return c // group if t == 0 else halves + c

    def sent(place, send, recv, sub):
        for p in range(halves):
            whole = win_a[p].at[pl.ds(place * owned, owned)]
            remote(whole, whole, send.at[p], recv.at[0, p * group], sub, fr).wait_send()
        for c in range(chunks):
            whole = slab(1, c, place)
            remote(whole, whole, send.at[halves + c], recv.at[1, c], sub, fr).wait_send()

    def cell(t, c, inner):
        if t == 0:
            return win_a[c // group].at[inner, within(c), :]
        return win_d[c].at[inner]

    def remote(src, dst, send, recv, sub, freq):
        return pltpu.make_async_remote_copy(
            src_ref=src,
            dst_ref=dst,
            send_sem=send,
            recv_sem=recv,
            device_id=(sub, freq),
            device_id_type=MESH,
        )

    own_copies = [
        [
            [
                pltpu.make_async_copy(
                    ref.at[here(c), pl.ds(inner * block, block)],
                    cell(t, c, inner),
                    own_sem.at[t, c],
                )
                for inner in range(owned)
            ]
            for c in range(chunks)
        ]
        for t, ref in enumerate((adj_hbm, dis_hbm))
    ]
    near_copies = [
        [
            remote(
                slab(t, c, 0), slab(t, c, 1), near_send.at[lot(t, c)], near_recv.at[t, c], partner, fr
            )
            for c in range(chunks)
        ]
        for t in range(2)
    ]
    relay_copies = [
        [
            remote(
                slab(t, c, 1), slab(t, c, 2), relay_send.at[lot(t, c)], relay_recv.at[t, c], target, fr
            )
            for c in range(chunks)
        ]
        for t in range(2)
    ]
    far_copies = [
        remote(far_out.at[c], far_in.at[c], far_send.at[0], far_recv.at[c], source, fr)
        for c in range(chunks)
    ]
    back_copies = [
        remote(near_out.at[c], near_in.at[c], back_send.at[0], back_recv.at[c], partner, fr)
        for c in range(chunks)
    ]
    peers = [(fr + d) % n_freq for d in range(n_freq)]
    pack_copies = [
        remote(pack.at[0], pack.at[d], pack_send.at[0], pack_recv.at[d - 1], me, peers[d])
        for d in range(1, n_freq)
    ]
    pair = pair_of(n_freq)
    teams = n_freq // pair
    team = fr // pair
    rank = fr % pair
    other = (rank + 1) % pair
    first_copies = [
        remote(
            first_out.at[s, other],
            first_in.at[s],
            first_send.at[0],
            first_recv.at[s],
            me,
            team * pair + other,
        )
        for s in range(sub_here)
    ]
    away = [(team + d) % teams for d in range(teams)]
    second_copies = [
        [
            remote(
                second_out.at[s, d - 1],
                second_in.at[s, d - 1],
                second_send.at[0],
                second_recv.at[s, d - 1],
                me,
                away[d] * pair + rank,
            )
            for d in range(1, teams)
        ]
        for s in range(sub_here)
    ]

    barrier = pltpu.get_barrier_semaphore()

    def greet(sub, freq):
        pl.semaphore_signal(barrier, inc=1, device_id=(sub, freq), device_id_type=MESH)

    greet(partner, fr)
    for d in range(1, n_freq):
        greet(me, peers[d])

    @pl.when(has_target)
    def _():
        greet(target, fr)

    @pl.when(has_source)
    def _():
        greet(source, fr)

    for copies in own_copies[0] + own_copies[1]:
        for copy in copies:
            copy.start()
    for copy in small_copies + weight_copies:
        copy.start()

    for ref in (*win_a, *win_d):
        ref[spare] = jnp.zeros(ref.shape[1:], ref.dtype)
    runs[n_slots] = jnp.zeros(runs.shape[1:], runs.dtype)
    flex_acc[...] = jnp.zeros_like(flex_acc)
    eig_acc[...] = jnp.zeros_like(eig_acc)

    with jax.named_scope("barrier"):
        pl.semaphore_wait(
            barrier, n_freq + has_target.astype(jnp.int32) + has_source.astype(jnp.int32)
        )
    def send(t):
        for c in range(chunks):
            pltpu.make_async_copy(slab(t, c, 0), slab(t, c, 0), own_sem.at[t, c]).wait()
            near_copies[t][c].start()

    leads = rank == 0
    follows = rank != 0

    @pl.when(leads)
    def _():
        send(0)
        send(1)

    def relay(t, c):
        with jax.named_scope(f"relay{t}{c}"):
            near_copies[t][c].wait_recv()

            @pl.when(has_target)
            def _():
                relay_copies[t][c].start()

    def relayed(t, c):
        with jax.named_scope(f"relayed{t}{c}"):

            @pl.when(has_source)
            def _():
                relay_copies[t][c].wait_recv()

    with jax.named_scope("small"):
        for copy in small_copies:
            copy.wait()

    one, none = jnp.int32(1), jnp.int32(0)
    keys = []
    for s in range(sub_here):
        for k in range(slots):
            named = inc_ref[s, k]
            live = k < count_ref[s]
            key = jnp.int32(spare)
            for w, owner in enumerate((me, partner, me - 1 + 2 * odd)):
                for inner in range(owned):
                    hit = live & (named == owner * owned + inner)
                    key = jnp.where(hit, jnp.int32(w * owned + inner), key)
            block_tab[s * slots + k] = key
            keys.append(key)

    def count(tests):
        total = none
        for test in tests:
            total = total + jnp.where(test, one, none)
        return total

    ranks = [
        count(
            [keys[j] <= keys[i] for j in range(i)]
            + [keys[j] < keys[i] for j in range(i + 1, n_slots)]
        )
        for i in range(n_slots)
    ]
    before = None
    for r in range(n_slots):
        index, key = none, none
        for i in range(n_slots):
            chosen = ranks[i] == r
            index = jnp.where(chosen, jnp.int32(i), index)
            key = jnp.where(chosen, keys[i], key)
        order_tab[r] = index
        if r:
            keep_tab[r] = jnp.where(key == before, jnp.float32(1), jnp.float32(0))
        before = key
    for b in range(3 * owned):
        hits = count([key == b for key in keys])
        upto = count([key <= b for key in keys])
        last_tab[b] = jnp.where(hits > 0, upto - 1, jnp.int32(n_slots))

    if pair > 1:

        @pl.when(follows)
        def _():
            send(0)

    for c in range(chunks):
        relay(0, c)
        if c == chunks - 1 and pair > 1:

            @pl.when(follows)
            def _():
                send(1)

    def gather(ref, s, where):
        return jnp.concatenate(
            [ref[block_tab[s * slots + k], where, :] for k in range(slots)],
            axis=1,
        )

    def scales(c, s):
        w2 = freq_ref[c]
        w4 = w2 * w2
        inverse = 1.0 / (eig_ref[pl.ds(s, 1), :] - w2)
        mode_index = lax.broadcasted_iota(jnp.int32, (1, modes), 1)
        factor = jnp.where(mode_index < mode_ref[s], w4 * inverse, 0.0)
        return w2, w4, inverse, factor

    tile = 2 * block if slots % 2 == 0 else block

    def respond(p):
        firsts, weights = [], []
        for s in range(sub_here):
            a = gather(win_a[p], s, pl.ds(0, group * rows))
            ma = dot(a, coup[s], NT)
            parts = []
            for i in range(group):
                c = p * group + i
                factor = scales(c, s)[3]
                piece = ma[i * rows : (i + 1) * rows]
                modal[s, here(c), :] = piece
                parts.append((-factor * piece).astype(jnp.bfloat16))
            wa = jnp.concatenate(parts, axis=0)
            weight_a[s, pl.ds(p * group * rows, group * rows), :] = wa
            firsts.append(a)
            weights.append(wa)
        for s in range(sub_here):
            a, wa = firsts[s], weights[s]
            if s == min(1, sub_here - 1) and p == halves - 1:
                pass_on(2)
            for n in range(kb // tile):
                lanes = slice(n * tile, (n + 1) * tile)
                plain = dot(a, stiff[s, lanes, :], NT) + dot(wa, coup[s, :, lanes], NN)
                inert = dot(a, mass[s, lanes, :], NT)
                for i in range(group):
                    c = p * group + i
                    w2, w4 = scales(c, s)[:2]
                    span = slice(i * rows, (i + 1) * rows)
                    value = (
                        plain[span]
                        - w2 * inert[span]
                        - (w4 * flex_ref[s : s + 1, lanes]) * a[span, lanes].astype(jnp.float32)
                    )
                    for k in range(tile // block):
                        slot = s * slots + n * (tile // block) + k
                        resp[slot, within(c), :] = value[:, k * block : (k + 1) * block]

    def spread(c):
        with jax.named_scope(f"spread{c}"):
            total = None
            for r in range(n_slots):
                term = resp[order_tab[r], within(c), :]
                total = term if total is None else total * keep_tab[r] + term
                runs[r] = total
            for place in (2, 1, 0):
                for inner in range(owned):
                    value = runs[last_tab[place * owned + inner]]
                    lane = pl.ds(inner * block, block)
                    if place == 0:
                        out_ref[here(c), lane] = value
                    elif place == 1:
                        near_acc[c, :, lane] = value
                    else:
                        far_out[c, :, lane] = value.astype(far_out.dtype)
                if place == 2:

                    @pl.when(has_source)
                    def _():
                        far_copies[c].start()

            @pl.when(jnp.logical_not(has_target))
            def _():
                near_out[c] = near_acc[c].astype(near_out.dtype)
                back_copies[c].start()

    def plan(c, stages):
        return stages[c * len(stages) // chunks]

    def pass_on(position):
        lead = [c for c in range(chunks) if plan(c, (0, 0, 1, 1)) == position]
        follow = [c for c in range(chunks) if plan(c, (1, 2, 2, 3)) == position]
        if pair == 1 or lead == follow:
            for c in lead:
                relay(1, c)
            return

        @pl.when(leads)
        def _():
            for c in lead:
                relay(1, c)

        @pl.when(follows)
        def _():
            for c in follow:
                relay(1, c)

    pass_on(0)
    for p in range(halves):
        for i in range(group):
            relayed(0, p * group + i)
        if p == 0:
            with jax.named_scope("weights"):
                for copy in weight_copies:
                    copy.wait()
        with jax.named_scope(f"respond{p}"):
            respond(p)
        for i in range(group):
            spread(p * group + i)
        if p == 0:
            pass_on(1)
    pass_on(3)

    def modal_part(c):
        lefts, rights = [], []
        for s in range(sub_here):
            w2, w4, inverse, factor = scales(c, s)
            d = gather(win_d[c], s, pl.ds(0, rows))
            a = gather(win_a[c // group], s, within(c))
            md = dot(d, coup[s], NT)
            wd = (-factor * md).astype(jnp.bfloat16)
            eig_acc[s] += (factor * inverse) * fold(modal[s, here(c), :] * md)
            lefts.append(jnp.concatenate([weight_a[s, here(c), :], wd], axis=0))
            rights.append(jnp.concatenate([d, a], axis=0))
        for s in range(sub_here):
            value = dot(lefts[s], rights[s], TN)
            if c:
                value = value + grad[s]
            grad[s] = value
            if c + 1 == chunks and pair > 1:
                for j in range(n_freq):
                    first_out[s, j % pair, j // pair] = value[
                        :, j * part : (j + 1) * part
                    ].astype(first_out.dtype)
        if c + 1 == chunks and pair > 1:
            for copy in first_copies:
                copy.start()

    def flex_part(c):
        w4 = freq_ref[c] * freq_ref[c]
        for place in range(3):
            for inner in range(owned):
                b = place * owned + inner
                a = win_a[c // group][b, within(c), :].astype(jnp.float32)
                d = win_d[c][b].astype(jnp.float32)
                flex_acc[b] += -w4 * fold(a * d)

    def combine(c, when=True):
        with jax.named_scope(f"combine{c}"):

            @pl.when(has_target & when)
            def _():
                far_copies[c].wait_recv()
                near_out[c] = (near_acc[c] + far_in[c].astype(jnp.float32)).astype(
                    near_out.dtype
                )
                back_copies[c].start()

    def finish(c):
        with jax.named_scope(f"finish{c}"):
            back_copies[c].wait_recv()
            out_ref[here(c), :] += near_in[c].astype(jnp.float32)

    combined = 0
    for c in range(chunks):
        relayed(1, c)
        with jax.named_scope(f"modal{c}"):
            modal_part(c)
        with jax.named_scope(f"flex{c}"):
            flex_part(c)
        if c == min(group, chunks) - 1:
            for i in range(group):
                combine(i, odd == 1)
            combined = group
        if c == chunks - 2:
            combine(0, odd == 0)
    for i in range(1 if chunks > 1 else 0, group):
        combine(i, odd == 0)

    with jax.named_scope("pack"):
        wide = max(block, modes)
        pack[0] = jnp.zeros(pack.shape[1:], pack.dtype)
        for s in range(sub_here):
            base = s * (slots + 1)
            for k in range(slots):
                pack[0, base + k : base + k + 1, 0:block] = jnp.sum(
                    flex_acc[block_tab[s * slots + k]], axis=0, keepdims=True
                )
            pack[0, base + slots : base + slots + 1, 0:modes] = jnp.sum(
                eig_acc[s], axis=0, keepdims=True
            )
        for copy in pack_copies:
            copy.start()

    for c in range(combined, chunks - 1):
        combine(c, odd == 1)

    for s in range(sub_here):
        with jax.named_scope(f"second{s}"):
            if pair > 1:
                first_copies[s].wait_recv()
            for d in range(1, teams):
                j = away[d]
                lane = pl.ds(pl.multiple_of((j * pair + rank) * part, part), part)
                value = grad[s, :, lane]
                if pair > 1:
                    value = value + first_in[s, j].astype(jnp.float32)
                second_out[s, d - 1] = value.astype(second_out.dtype)
            for copy in second_copies[s]:
                copy.start()

    for c in range(combined, chunks - 1):
        combine(c, odd == 0)
    for c in range(max(combined, chunks - 1), chunks):
        combine(c)

    for c in range(chunks):
        finish(c)

    with jax.named_scope("packwait"):
        for copy in pack_copies:
            copy.wait_recv()
    total = None
    for i in range(n_freq):
        term = pack[(fr - i + n_freq) % n_freq]
        total = term if total is None else total + term
    for s in range(sub_here):
        base = s * (slots + 1)
        for k in range(slots):
            flex_out[s : s + 1, k * block : (k + 1) * block] = total[
                base + k : base + k + 1, 0:block
            ]
        eig_out[s : s + 1, :] = total[base + slots : base + slots + 1, 0:modes]
    for s in range(sub_here):
        with jax.named_scope(f"grad{s}"):
            lane = pl.ds(pl.multiple_of(fr * part, part), part)
            value = grad[s, :, lane]
            if pair > 1:
                value = value + first_in[s, team].astype(jnp.float32)
            for d in range(1, teams):
                second_copies[s][d - 1].wait_recv()
                value = value + second_in[s, d - 1].astype(jnp.float32)
            cg_out_ref[s] = value

    with jax.named_scope("end"):
        sent(0, near_send, near_recv, partner)
        remote(near_out, near_in, back_send.at[0], back_recv.at[0], partner, fr).wait_send()

        @pl.when(has_target)
        def _():
            sent(1, relay_send, relay_recv, target)

        @pl.when(has_source)
        def _():
            remote(far_out, far_in, far_send.at[0], far_recv.at[0], source, fr).wait_send()

        if n_freq > 1:
            whole = pack.at[pl.ds(1, n_freq - 1)]
            remote(whole, whole, pack_send.at[0], pack_recv.at[0], me, peers[1]).wait_send()
        if pair > 1:
            remote(
                first_out.at[pl.ds(0, sub_here), other],
                first_in,
                first_send.at[0],
                first_recv.at[0],
                me,
                team * pair + other,
            ).wait_send()
        if teams > 1:
            remote(
                second_out,
                second_in,
                second_send.at[0],
                second_recv.at[0, 0],
                me,
                away[1] * pair + rank,
            ).wait_send()


def write_out(*refs):
    count = len(refs) // 2
    sems = refs[-1]
    copies = [
        pltpu.make_async_copy(refs[i], refs[count + i], sems.at[i]) for i in range(count)
    ]
    for copy in copies:
        copy.start()
    for copy in copies:
        copy.wait()


def shards(
    n_sub,
    n_freq,
    freq_squared,
    displacement,
    adjoint,
    incidence,
    block_count,
    mode_count,
    stiffness,
    mass_matrix,
    coupling,
    eigenvalues,
    flexibility,
):
    sub_here, slots = incidence.shape
    columns, owned_cells = displacement.shape
    chunks = freq_squared.shape[0]
    rows = columns // chunks
    kb = stiffness.shape[1]
    block = kb // slots
    owned = owned_cells // block
    modes = coupling.shape[1]
    part = kb // n_freq
    group = group_of(chunks)
    pair = pair_of(n_freq)
    teams = n_freq // pair
    n_slots = sub_here * slots
    pack_rows = -(-(sub_here * (slots + 1)) // 8) * 8
    bf16, f32, i32 = jnp.bfloat16, jnp.float32, jnp.int32
    vmem = pl.BlockSpec(memory_space=pltpu.VMEM)
    hbm = pl.BlockSpec(memory_space=pltpu.HBM)
    dma = pltpu.SemaphoreType.DMA
    slab = (chunks, rows, owned_cells)
    scratch = (
        [
            pltpu.VMEM((3 * owned + 1, group * rows, block), bf16)
            for _ in range(chunks // group)
        ]
        + [pltpu.VMEM((3 * owned + 1, rows, block), bf16) for _ in range(chunks)]
        + [
            pltpu.SMEM(freq_squared.shape, f32),
            pltpu.SMEM(incidence.shape, i32),
            pltpu.SMEM(block_count.shape, i32),
            pltpu.SMEM(mode_count.shape, i32),
            pltpu.SMEM((n_slots,), i32),
            pltpu.SMEM((n_slots,), i32),
            pltpu.SMEM((3 * owned,), i32),
            pltpu.SMEM((n_slots,), f32),
            pltpu.VMEM(eigenvalues.shape, f32),
            pltpu.VMEM(flexibility.shape, f32),
            pltpu.VMEM(stiffness.shape, bf16),
            pltpu.VMEM(mass_matrix.shape, bf16),
            pltpu.VMEM(coupling.shape, bf16),
            pltpu.VMEM((n_slots, group * rows, block), f32),
            pltpu.VMEM((n_slots + 1, rows, block), f32),
            pltpu.VMEM((sub_here, columns, modes), f32),
            pltpu.VMEM((sub_here, columns, modes), bf16),
            pltpu.VMEM(slab, f32),
            pltpu.VMEM(slab, bf16),
            pltpu.VMEM(slab, bf16),
            pltpu.VMEM(slab, bf16),
            pltpu.VMEM(slab, bf16),
            pltpu.VMEM((3 * owned + 1, 8, block), f32),
            pltpu.VMEM((sub_here, 8, modes), f32),
            pltpu.VMEM((n_freq, pack_rows, max(block, modes)), f32),
            pltpu.VMEM((sub_here, modes, kb), f32),
            pltpu.VMEM((sub_here, pair, teams, modes, part), bf16),
            pltpu.VMEM((sub_here, teams, modes, part), bf16),
            pltpu.VMEM((sub_here, max(teams - 1, 1), modes, part), bf16),
            pltpu.VMEM((sub_here, max(teams - 1, 1), modes, part), bf16),
            dma((2, chunks)),
            dma((3,)),
            dma((6,)),
            dma((chunks // group + chunks,)),
            dma((2, chunks)),
            dma((chunks // group + chunks,)),
            dma((2, chunks)),
            dma((1,)),
            dma((chunks,)),
            dma((1,)),
            dma((chunks,)),
            dma((1,)),
            dma((max(n_freq - 1, 1),)),
            dma((1,)),
            dma((sub_here,)),
            dma((1,)),
            dma((sub_here, max(teams - 1, 1))),
        ]
    )
    results = pl.pallas_call(
        functools.partial(kernel, n_sub, n_freq, chunks),
        out_shape=(
            jax.ShapeDtypeStruct((columns, owned_cells), f32),
            jax.ShapeDtypeStruct((sub_here, modes), f32),
            jax.ShapeDtypeStruct((sub_here, modes, part), f32),
            jax.ShapeDtypeStruct((sub_here, kb), f32),
        ),
        in_specs=[hbm] * 11,
        out_specs=(vmem,) * 4,
        scratch_shapes=scratch,
        compiler_params=pltpu.CompilerParams(
            collective_id=0, has_side_effects=True, vmem_limit_bytes=48 * 1024 * 1024
        ),
    )(
        *(
            pltpu.with_memory_space_constraint(x, pltpu.HBM)
            for x in (
                freq_squared,
                incidence,
                block_count,
                mode_count,
                eigenvalues,
                flexibility,
                adjoint,
                displacement,
                stiffness,
                mass_matrix,
                coupling,
            )
        )
    )
    return pl.pallas_call(
        write_out,
        out_shape=tuple(jax.ShapeDtypeStruct(x.shape, x.dtype) for x in results),
        in_specs=[vmem] * 4,
        out_specs=(pl.BlockSpec(memory_space=pltpu.HBM),) * 4,
        scratch_shapes=[dma((4,))],
        compiler_params=pltpu.CompilerParams(vmem_limit_bytes=4 * 1024 * 1024),
    )(*results)


def solution(mesh):
    in_specs = (
        P("freq"),
        P("freq", "sub"),
        P("freq", "sub"),
        P("sub", None),
        P("sub"),
        P("sub"),
        P("sub", None, None),
        P("sub", None, None),
        P("sub", None, None),
        P("sub", None),
        P("sub", None),
    )
    out_specs = (P("freq", "sub"), P("sub", None), P("sub", None, "freq"), P("sub", None))
    body = functools.partial(shards, mesh.shape["sub"], mesh.shape["freq"])
    return jax.shard_map(body, mesh=mesh, in_specs=in_specs, out_specs=out_specs, check_vma=False)
```
